256 devices in a mesh: rows: 32 (over z, x), far: 8 (over y, core).
Axes of the slice: x: 4, y: 4, z: 8, core: 2. Of those that a mesh axis runs over, the one named last changes fastest.
Arguments:
- right_side: float32 [65536, 256], P('rows'), may hold values from -24 to 24
- near_blocks: float32 [512, 48, 128, 128], P('rows', 'far'), may hold values from -0.0234375 to 0.0234375
- near_cols: int32 [512, 48], P('rows', 'far'), may hold values from 0 to 511, as said below
- far_src: int32 [32, 32, 8], P('rows', None, 'far'), may hold values from 0 to 15
- far_tgt: int32 [32, 32, 8], P('rows', None, 'far'), may hold values from 0 to 15
- far_left: float32 [32, 32, 8, 128, 64], P('rows', None, 'far'), may hold values from -0.0546875 to 0.0546875
- far_right: float32 [32, 32, 8, 128, 64], P('rows', None, 'far'), may hold values from -0.5 to 0.5
Outputs:
- solution: float32 [65536, 256], P('rows', 'far')
- residual: float32 [65536, 256], P('rows', 'far')
The draws below stay inside these ranges and needn't reach their ends.
Inputs may be any that keep to these rules, and one draw needn't show every extreme that they name: `near_cols`: each near-field column lies within 8 clusters of its row; slot 0 of row i names i itself, slot 1 names min(i + 8, 511) and slot 2 names max(i - 8, 0).
All inputs are finite; a program needn't handle non-finite values.
Results may differ from the reference program's by a relative error of at most 0.0003.
Values sent between devices are 32-bit elements; how exact they have to be, the bound alone decides.
A program may use at most 128 MiB of HBM per device.

```python
import jax
import jax.numpy as jnp
from jax import lax

B = 128
R = 64
NRHS = 256
CL_DEV = 16
REACH = 8
NC = 512
PANELS = 65536
NEAR = 48
FSLOT = 8
N_ROWS = 32


def draw_right_side(key, part):
    ramp = 1.0 + 2.0 * jnp.arange(PANELS, dtype=jnp.float32) / (PANELS - 1)
    values = jnp.clip(jax.random.normal(key, (PANELS, NRHS), jnp.float32), -4.0, 4.0)
    return values * ramp[:, None]


def draw_near_cols(key, part):
    row_ids = jnp.arange(NC, dtype=jnp.int32)[:, None]
    jumps = jax.random.randint(key, (NC, NEAR), -REACH, REACH + 1, jnp.int32)
    slot_ids = jnp.arange(NEAR, dtype=jnp.int32)[None, :]
    jumps = jnp.where(slot_ids == 0, 0, jnp.where(slot_ids == 1, REACH, jnp.where(slot_ids == 2, -REACH, jumps)))
    return jnp.clip(row_ids + jumps, 0, NC - 1).astype(jnp.int32)


def touch_ends(values, key, low, top_value):
    longest = values.shape.index(max(values.shape))
    spots = []
    for shift in (0, 1):
        where = [jax.random.randint(jax.random.fold_in(key, axis), (), 0, length) for axis, length in enumerate(values.shape)]
        where[longest] = (where[longest] + shift) % values.shape[longest]
        spots.append(tuple(where))
    return values.at[spots[0]].set(low).at[spots[1]].set(top_value)


def steps_of(own_key, extent, shards, low, largest):
    level = 1.0
    for position, shards_of in shards:
        steps = jax.random.uniform(jax.random.fold_in(jax.random.fold_in(own_key, 6), position), (shards_of,), jnp.float32, low / len(shards), largest / len(shards))
        level = level * jnp.repeat(jnp.exp(steps), extent[position] // shards_of).reshape((-1,) + (1,) * (len(extent) - 1 - position))
    return level


def centred(key, shape, deviation, limit, cuts=(), kind=jnp.bfloat16):
    array = jax.random.normal(key, shape, jnp.float32) * deviation
    if len(cuts) > 0:
        array = steps_of(key, shape, cuts, -0.22, 0.18) * array
    return jnp.clip(array, min=-limit, max=limit).astype(kind)


def setup_inputs(seed: int = 0) -> dict:
    streams_of = jax.random.split(jax.random.key(seed), 8)
    right_side = draw_right_side(jax.random.fold_in(streams_of[7], 71), 0)
    near_blocks = centred(streams_of[1], (NC, NEAR, B, B), (12 * B * NEAR) ** -0.5, 0.0234375, ((0, 32), (1, 8)), jnp.float32)
    near_cols = draw_near_cols(jax.random.fold_in(streams_of[7], 71), 0)
    far_src = touch_ends(jax.random.randint(streams_of[3], (N_ROWS, N_ROWS, FSLOT), 0, CL_DEV), jax.random.fold_in(streams_of[3], 1), 0, CL_DEV - 1).astype(jnp.int32)
    far_tgt = touch_ends(jax.random.randint(streams_of[4], (N_ROWS, N_ROWS, FSLOT), 0, CL_DEV), jax.random.fold_in(streams_of[4], 1), 0, CL_DEV - 1).astype(jnp.int32)
    far_left = centred(streams_of[5], (N_ROWS, N_ROWS, FSLOT, B, R), (11 * R * N_ROWS * FSLOT // CL_DEV) ** -0.5, 0.0546875, ((0, 32), (2, 8)), jnp.float32)
    far_right = centred(streams_of[6], (N_ROWS, N_ROWS, FSLOT, B, R), B ** -0.5, 0.5, ((0, 32), (2, 8)), jnp.float32)
    return {"right_side": right_side, "near_blocks": near_blocks, "near_cols": near_cols, "far_src": far_src, "far_tgt": far_tgt, "far_left": far_left, "far_right": far_right}


TOP_PRECISION = lax.Precision.HIGHEST
EPS = 1e-06

def column_dots(left_vec, right_vector):
    return lax.optimization_barrier(jnp.sum(left_vec * right_vector, axis=0))

def apply_operator(vector_in, near_blocks, near_cols, far_src, far_tgt, far_left, far_right):
    blocks = vector_in.reshape(NC, B, NRHS)

    def nearby_group(items):
        group_blocks, group_columns = items
        picked = jnp.take(blocks, group_columns, axis=0)
        return jnp.einsum('cspq,csqn->cpn', group_blocks, picked, precision=TOP_PRECISION)
    near_part = lax.map(nearby_group, (near_blocks.reshape(N_ROWS, CL_DEV, NEAR, B, B), near_cols.reshape(N_ROWS, CL_DEV, NEAR)))
    starts = (jnp.arange(N_ROWS, dtype=jnp.int32) * CL_DEV)[:, None]
    columns = jnp.arange(CL_DEV, dtype=jnp.int32)

    def far_group(triple):
        target, left_here, target_local = triple
        src_here = lax.dynamic_index_in_dim(far_src, target, 1, keepdims=False)
        right_here = lax.dynamic_index_in_dim(far_right, target, 1, keepdims=False)
        picked = jnp.take(blocks, src_here + starts, axis=0)
        coefficients = jnp.einsum('asbr,asbn->asrn', right_here, picked, precision=TOP_PRECISION)
        contribution_part = jnp.einsum('asbr,asrn->asbn', left_here, coefficients, precision=TOP_PRECISION)
        owning_devices = (target_local[:, :, None] == columns).astype(jnp.float32)
        return jnp.einsum('hyo,hyze->oze', owning_devices, contribution_part, precision=TOP_PRECISION)
    far_part = lax.map(far_group, (jnp.arange(N_ROWS, dtype=jnp.int32), far_left, far_tgt))
    return 0.5 * vector_in + (near_part + far_part).reshape(PANELS, NRHS)

def least_squares(rhs_length, upper_left, lower_left, column_two, lower_right):
    radius_one = jnp.sqrt(upper_left * upper_left + lower_left * lower_left)
    cosine_one = upper_left / radius_one
    sine_one = lower_left / radius_one
    rotated_top = cosine_one * rhs_length
    rotated_mid = -sine_one * rhs_length
    coupled = cosine_one * column_two[0] + sine_one * column_two[1]
    diagonal_two = cosine_one * column_two[1] - sine_one * column_two[0]
    radius_two = jnp.sqrt(diagonal_two * diagonal_two + lower_right * lower_right)
    weight_two = diagonal_two * rotated_mid / (radius_two * radius_two)
    weight_one = (rotated_top - coupled * weight_two) / radius_one
    return (weight_one, weight_two)

def reference(right_side, near_blocks, near_cols, far_src, far_tgt, far_left, far_right):

    def apply_op(vector_in):
        return apply_operator(vector_in, near_blocks, near_cols, far_src, far_tgt, far_left, far_right)
    rhs_length = jnp.sqrt(column_dots(right_side, right_side) + EPS)
    first_vector = right_side / rhs_length
    image_one = apply_op(first_vector)
    upper_left = column_dots(first_vector, image_one)
    candidate = image_one - upper_left * first_vector
    lower_left = jnp.sqrt(column_dots(candidate, candidate) + EPS)
    second_vec = candidate / lower_left
    image_two = apply_op(second_vec)
    column_two = (column_dots(first_vector, image_two), column_dots(second_vec, image_two))
    candidate = image_two - column_two[0] * first_vector
    candidate = candidate - column_two[1] * second_vec
    lower_right = jnp.sqrt(column_dots(candidate, candidate) + EPS)
    weight_one, weight_two = least_squares(rhs_length, upper_left, lower_left, column_two, lower_right)
    solution = weight_one * first_vector + weight_two * second_vec
    residual = right_side - apply_op(solution)
    return (solution, residual)
```

```python
import jax
import jax.numpy as jnp
from jax import lax
from jax.sharding import PartitionSpec as P

B = 128
CL_DEV = 16
REACH = 8


TOP_PRECISION = lax.Precision.HIGHEST
EPS = 1e-06


def with_halo(cells, sides, width):
    for axis, dim in sides:
        count = lax.axis_size(axis)
        ends = count - 1
        head = lax.slice_in_dim(cells, 0, width, axis=dim)
        tail = lax.slice_in_dim(cells, cells.shape[dim] - width, cells.shape[dim], axis=dim)
        cells = jnp.concatenate(
            [
                lax.ppermute(tail, axis, [(i, (i + 1) % count) for i in range(ends)]),
                cells,
                lax.ppermute(head, axis, [((i + 1) % count, i) for i in range(ends)]),
            ],
            axis=dim,
        )
    return cells


def column_dots(left_vec, right_vector):
    return jnp.sum(left_vec * right_vector, axis=0)


def near_term(vector_in, near_blocks, near_cols):
    rhs_count = vector_in.shape[1]
    padded = with_halo(vector_in, (("rows", 0),), REACH * B)
    clusters = padded.reshape(-1, B, rhs_count)
    offset = lax.axis_index("rows") * CL_DEV - REACH
    picked = jnp.take(clusters, near_cols - offset, axis=0)
    return jnp.einsum("cspq,csqn->cpn", near_blocks, picked, precision=TOP_PRECISION)


def far_term(vector_in, far_src, far_tgt, far_left, far_right):
    clusters = vector_in.reshape(CL_DEV, B, vector_in.shape[1])
    picked = jnp.take(clusters, far_src[0], axis=0)
    coefficients = jnp.einsum("tsbr,tsbn->tsrn", far_right[0], picked, precision=TOP_PRECISION)
    owning_devices = (far_tgt[0][:, :, None] == jnp.arange(CL_DEV, dtype=jnp.int32)).astype(
        jnp.float32
    )
    contribution_part = jnp.einsum(
        "asbr,asrn->asbn",
        far_left[0],
        lax.all_to_all(coefficients, "rows", split_axis=0, concat_axis=0, tiled=True),
        precision=TOP_PRECISION,
    )
    return jnp.einsum("hyo,hyze->oze", owning_devices, contribution_part, precision=TOP_PRECISION)


def own_columns(vector_in):
    share_width = vector_in.shape[-1] // lax.axis_size("far")
    return lax.dynamic_slice_in_dim(
        vector_in, lax.axis_index("far") * share_width, share_width, vector_in.ndim - 1
    )


def combine(gram):
    bb, bu, uu, bw, uw, ww = gram
    length_sq = bb + EPS
    length = jnp.sqrt(length_sq)
    unit = bb / length_sq
    gap = EPS / length_sq
    p1, q11, p2, q12, q22 = bu / length_sq, uu / length_sq, bw / length_sq, uw / length_sq, ww / length_sq
    upper_left = 0.5 * unit + p1
    alpha = p1 - 0.5 * gap
    cand_sq = jnp.maximum(q11 - 2.0 * alpha * p1 + alpha * alpha * unit, 0.0)
    lower_sq = cand_sq + EPS
    lower_left = jnp.sqrt(lower_sq)
    f_s = (p1 - alpha * unit) / lower_left
    f_ns = (p2 - alpha * p1) / lower_left
    s_s = cand_sq / lower_sq
    s_ns = (q12 - alpha * q11 - alpha * p2 + alpha * alpha * p1) / lower_sq
    ns_ns = (q22 - 2.0 * alpha * q12 + alpha * alpha * q11) / lower_sq
    top = 0.5 * f_s + f_ns
    mid = 0.5 * s_s + s_ns
    beta = s_ns - 0.5 * EPS / lower_sq
    rest_sq = ns_ns + top * top * unit + beta * beta * s_s - 2.0 * top * f_ns - 2.0 * beta * s_ns + 2.0 * top * beta * f_s
    lower_right = jnp.sqrt(jnp.maximum(rest_sq, 0.0) + EPS)
    radius_one = jnp.sqrt(upper_left * upper_left + lower_left * lower_left)
    cosine_one = upper_left / radius_one
    sine_one = lower_left / radius_one
    rotated_top = cosine_one * length
    rotated_mid = -sine_one * length
    coupled = cosine_one * top + sine_one * mid
    diagonal_two = cosine_one * mid - sine_one * top
    radius_two = jnp.sqrt(diagonal_two * diagonal_two + lower_right * lower_right)
    weight_two = diagonal_two * rotated_mid / (radius_two * radius_two)
    weight_one = (rotated_top - coupled * weight_two) / radius_one
    one = weight_one / length
    two = weight_two / (lower_left * length)
    sol_b = one - alpha * two
    return sol_b, two, 1.0 - 0.5 * sol_b, -0.5 * two - one + alpha * two, -two


def shards(right_side, near_blocks, near_cols, far_src, far_tgt, far_left, far_right):

    def partial_image(vector_in):
        near_part = near_term(vector_in, near_blocks, near_cols)
        far_part = far_term(vector_in, far_src, far_tgt, far_left, far_right)
        return (near_part + far_part).reshape(vector_in.shape)

    image_one = lax.psum(partial_image(right_side), "far")
    own_two = lax.psum_scatter(partial_image(image_one), "far", scatter_dimension=1, tiled=True)
    own_side = own_columns(right_side)
    own_one = own_columns(image_one)
    pairs = ((own_side, own_side), (own_side, own_one), (own_one, own_one), (own_side, own_two), (own_one, own_two), (own_two, own_two))
    gram = lax.psum(jnp.stack([column_dots(left, right) for left, right in pairs]), "rows")
    sol_b, sol_u, res_b, res_u, res_w = combine(gram)
    return (sol_b * own_side + sol_u * own_one, res_b * own_side + res_u * own_one + res_w * own_two)


def solution(mesh):
    return jax.shard_map(
        shards,
        mesh=mesh,
        in_specs=(
            P("rows", None),
            P("rows", "far", None, None),
            P("rows", "far"),
            P("rows", None, "far"),
            P("rows", None, "far"),
            P("rows", None, "far", None, None),
            P("rows", None, "far", None, None),
        ),
        out_specs=(P("rows", "far"), P("rows", "far")),
        check_vma=False,
    )
```

```python
import functools

import jax
import jax.numpy as jnp
from jax import lax
from jax.experimental import pallas as pl
from jax.experimental.pallas import tpu as pltpu
from jax.sharding import PartitionSpec as P

B = 128
R = 64
HALF = 128
NEAR_DEV = 6
CL_DEV = 16
ROW_X = 4
FAR_Y = 4
EPS = 1e-06
MESH = pl.DeviceIdType.MESH
F32 = jnp.float32
BF16 = jnp.bfloat16


def split(value):
    high = value.astype(BF16)
    return high, (value - high.astype(F32)).astype(BF16)


def quadrants(value):
    rows = value.shape[0] // 2
    return (value[:rows, :HALF] + value[:rows, HALF:]) + (value[rows:, :HALF] + value[rows:, HALF:])


def combine(gram):
    bb, bu, uu, bw, uw, ww = gram
    length_sq = bb + EPS
    length = jnp.sqrt(length_sq)
    unit = bb / length_sq
    gap = EPS / length_sq
    p1, q11, p2, q12, q22 = bu / length_sq, uu / length_sq, bw / length_sq, uw / length_sq, ww / length_sq
    upper_left = 0.5 * unit + p1
    alpha = p1 - 0.5 * gap
    cand_sq = jnp.maximum(q11 - 2.0 * alpha * p1 + alpha * alpha * unit, 0.0)
    lower_sq = cand_sq + EPS
    lower_left = jnp.sqrt(lower_sq)
    f_s = (p1 - alpha * unit) / lower_left
    f_ns = (p2 - alpha * p1) / lower_left
    s_s = cand_sq / lower_sq
    s_ns = (q12 - alpha * q11 - alpha * p2 + alpha * alpha * p1) / lower_sq
    ns_ns = (q22 - 2.0 * alpha * q12 + alpha * alpha * q11) / lower_sq
    top = 0.5 * f_s + f_ns
    mid = 0.5 * s_s + s_ns
    beta = s_ns - 0.5 * EPS / lower_sq
    rest_sq = ns_ns + top * top * unit + beta * beta * s_s - 2.0 * top * f_ns - 2.0 * beta * s_ns + 2.0 * top * beta * f_s
    lower_right = jnp.sqrt(jnp.maximum(rest_sq, 0.0) + EPS)
    radius_one = jnp.sqrt(upper_left * upper_left + lower_left * lower_left)
    cosine_one = upper_left / radius_one
    sine_one = lower_left / radius_one
    rotated_top = cosine_one * length
    rotated_mid = -sine_one * length
    coupled = cosine_one * top + sine_one * mid
    diagonal_two = cosine_one * mid - sine_one * top
    radius_two = jnp.sqrt(diagonal_two * diagonal_two + lower_right * lower_right)
    weight_two = diagonal_two * rotated_mid / (radius_two * radius_two)
    weight_one = (rotated_top - coupled * weight_two) / radius_one
    one = weight_one / length
    two = weight_two / (lower_left * length)
    sol_b = one - alpha * two
    return sol_b, two, 1.0 - 0.5 * sol_b, -0.5 * two - one + alpha * two, -two


def kernel(
    n_rows,
    cols_ref, src_ref, tgt_ref, side_hbm, near_hbm, left_hbm, right_hbm,
    sol_ref, res_ref,
    side, near_raw, near, left_raw, left, right_raw, right, vcat, coef_out, coef_in,
    halo_b, own_u, halo_u, acc, chain, part, part_t,
    sib_in, mix, y_in, sib_t, mix_t, y_t, turned, own_w, gram_out, gram_in,
    prev, last,
    load_sem, a2a_s, a2a_r, halo_s, halo_r, agy_s, agy_r, ags_s, ags_r,
    rss_s, rss_r, rsy_s, rsy_r, rts_s, rts_r, rty_s, rty_r, gram_s, gram_r,
):
    n_z = n_rows // ROW_X
    me = lax.axis_index("rows")
    far = lax.axis_index("far")
    my_x, my_z = lax.rem(me, ROW_X), lax.div(me, ROW_X)
    my_y, my_c = lax.div(far, 2), lax.rem(far, 2)
    sib = my_y * 2 + 1 - my_c

    def ahead(k):
        return lax.rem(my_z + lax.div(k, ROW_X), n_z) * ROW_X + lax.rem(my_x + lax.rem(k, ROW_X), ROW_X)

    def behind(k):
        return lax.rem(my_z + n_z - lax.div(k, ROW_X), n_z) * ROW_X + lax.rem(my_x + ROW_X - lax.rem(k, ROW_X), ROW_X)

    def y_peer(d):
        return lax.rem(my_y + d, FAR_Y) * 2 + my_c

    def y_from(d):
        return lax.rem(my_y + FAR_Y - d, FAR_Y) * 2 + my_c

    def remote(src, dst, send, recv, rows, to_far):
        return pltpu.make_async_remote_copy(
            src_ref=src, dst_ref=dst, send_sem=send, recv_sem=recv,
            device_id={"rows": rows, "far": to_far}, device_id_type=MESH,
        )

    loads = [
        pltpu.make_async_copy(side_hbm, side, load_sem.at[0]),
        pltpu.make_async_copy(right_hbm, right_raw, load_sem.at[1]),
        pltpu.make_async_copy(left_hbm, left_raw, load_sem.at[2]),
        pltpu.make_async_copy(near_hbm, near_raw, load_sem.at[3]),
    ]
    for load in loads:
        load.start()

    barrier = pltpu.get_barrier_semaphore()

    def greet(k, carry):
        pl.semaphore_signal(barrier, inc=1, device_id={"rows": ahead(k), "far": far}, device_id_type=MESH)
        return carry

    lax.fori_loop(1, n_rows, greet, 0)
    for d in (1, 2, 3):
        pl.semaphore_signal(barrier, inc=1, device_id={"rows": me, "far": y_peer(d)}, device_id_type=MESH)
    pl.semaphore_signal(barrier, inc=1, device_id={"rows": me, "far": sib}, device_id_type=MESH)

    loads[0].wait()

    def put(q, slot, value):
        high, low = split(value)
        vcat[q, slot, :, :HALF] = high
        vcat[q, slot, :, HALF:] = low

    def take_side(o, carry):
        put(0, o + 8, side[o, :, :HALF])
        put(1, o + 8, side[o, :, HALF:])
        return carry

    lax.fori_loop(0, CL_DEV, take_side, 0)
    loads[1].wait()

    def take_right(t, carry):
        high, low = split(right_raw[t])
        right[t, :R, :] = high
        right[t, R:, :] = low
        return carry

    lax.fori_loop(0, n_rows, take_right, 0)
    pl.semaphore_wait(barrier, n_rows + 3)

    halo_to = lax.rem(me + n_rows - 1 + 2 * lax.div(far, 4), n_rows)

    def halo_copy(g):
        if g == 0:
            return remote(side_hbm.at[pl.ds(2 * far, 2)], halo_b.at[far], halo_s.at[0], halo_r.at[0], halo_to, far)
        return remote(own_u.at[g - 1, far], halo_u.at[g - 1, far], halo_s.at[g], halo_r.at[g], halo_to, far)

    halo_copy(0).start()

    def a2a(ap, q, k):
        return remote(coef_out.at[ap, q, k], coef_in.at[ap, q, k], a2a_s.at[ap, q, k], a2a_r.at[ap, q, k], ahead(k), far)

    def coefficient(q, t):
        return quadrants(jnp.dot(right[t], vcat[q, src_ref[t] + 8], preferred_element_type=F32))

    def send_coefficients(ap, q):
        def step(k, carry):
            coef_out[ap, q, k] = coefficient(q, ahead(k))
            a2a(ap, q, k).start()
            return carry

        lax.fori_loop(1, n_rows, step, 0)
        coef_in[ap, q, 0] = coefficient(q, me)

    send_coefficients(0, 0)
    send_coefficients(0, 1)

    def group_ref(g, who):
        if g == 0:
            return halo_b.at[who]
        if g <= 2:
            return own_u.at[g - 1, who]
        return halo_u.at[g - 3, who]

    def gather_y(g, d):
        ref = group_ref(g, far)
        return remote(ref, ref, agy_s.at[g, d], agy_r.at[g, d], me, y_peer(d))

    def gather_sib(g, d):
        ref = group_ref(g, y_from(d))
        return remote(ref, ref, ags_s.at[g, d], ags_r.at[g, d], me, sib)

    def gather_start(g):
        for d in (2, 1, 3):
            gather_y(g, d).start()
        gather_sib(g, 0).start()

    def gather_forward(g):
        for d in (1, 3, 2):
            ref = group_ref(g, y_from(d))
            remote(ref, ref, agy_s.at[g, d], agy_r.at[g, d], me, y_peer(d)).wait_recv()
            gather_sib(g, d).start()

    def gather_end(g):
        for d in range(FAR_Y):
            ref = group_ref(g, lax.rem(my_y + FAR_Y - d, FAR_Y) * 2 + 1 - my_c)
            remote(ref, ref, ags_s.at[g, d], ags_r.at[g, d], me, sib).wait_recv()

    halo_copy(0).wait_recv()
    gather_start(0)

    def tables(k, carry):
        mine = tgt_ref[behind(k)]
        found = n_rows
        for j in range(n_rows):
            same = jnp.logical_and(tgt_ref[behind(j)] == mine, j < k)
            found = jnp.where(same, j, found)
        prev[k] = found
        return carry

    lax.fori_loop(0, n_rows, tables, 0)

    def ends(o, carry):
        found = n_rows
        for j in range(n_rows):
            found = jnp.where(tgt_ref[behind(j)] == o, j, found)
        last[o] = found
        return carry

    lax.fori_loop(0, CL_DEV, ends, 0)
    chain[n_rows] = jnp.zeros((B, HALF), F32)
    loads[2].wait()

    def take_left(a, carry):
        high, low = split(left_raw[a].T)
        left[a, :B, :] = high
        left[a, B:, :] = low
        return carry

    lax.fori_loop(0, n_rows, take_left, 0)
    gather_forward(0)
    loads[3].wait()

    def take_near(o, carry):
        for s in range(NEAR_DEV):
            high, low = split(near_raw[o, s])
            near[o, :B, s * B : (s + 1) * B] = high
            near[o, B:, s * B : (s + 1) * B] = low
        return carry

    lax.fori_loop(0, CL_DEV, take_near, 0)
    gather_end(0)

    def take_halo_b(j, carry):
        who, i = lax.div(j, 2), lax.rem(j, 2)
        slot = lax.rem(j + 24, 32)
        put(0, slot, halo_b[who, i, :, :HALF])
        put(1, slot, halo_b[who, i, :, HALF:])
        return carry

    lax.fori_loop(0, CL_DEV, take_halo_b, 0)
    base = me * CL_DEV - 8

    def near_term(q):
        def step(o, carry):
            picked = [vcat[q, jnp.clip(cols_ref[s, o] - base, 0, 31)] for s in range(NEAR_DEV)]
            acc[q, o] = quadrants(jnp.dot(near[o], jnp.concatenate(picked, axis=0), preferred_element_type=F32))
            return carry

        lax.fori_loop(0, CL_DEV, step, 0)

    def far_term(ap, q, first, end):
        def step(k, carry):
            a2a_in = remote(coef_out.at[ap, q, k], coef_in.at[ap, q, k], a2a_s.at[ap, q, k], a2a_r.at[ap, q, k], ahead(k), far)
            a2a_in.wait_recv()
            add(ap, q, k)
            return carry

        def add(ap, q, k):
            both = jnp.concatenate(split(coef_in[ap, q, k]), axis=1)
            here = quadrants(jnp.dot(left[behind(k)], both, preferred_element_type=F32))
            chain[k] = here + chain[prev[k]]

        if first == 0:
            add(ap, q, 0)
        lax.fori_loop(max(first, 1), end, step, 0)

    near_term(0)
    near_term(1)
    far_term(0, 0, 0, n_rows)

    def finish_rows(q):
        def step(o, carry):
            part[q, lax.div(o, 4), lax.rem(lax.div(o, 2), 2), lax.rem(o, 2)] = acc[q, o] + chain[last[o]]
            return carry

        lax.fori_loop(0, CL_DEV, step, 0)

    def rows_sib(q):
        return remote(part.at[q, :, 1 - my_c], sib_in.at[q], rss_s.at[q], rss_r.at[q], me, sib)

    def rows_y(q, d):
        return remote(mix.at[q, d], y_in.at[q, d], rsy_s.at[q, d], rsy_r.at[q, d], me, y_peer(d))

    def rows_send(q):
        for d in (2, 1, 3):
            to_y = lax.rem(my_y + d, FAR_Y)
            mix[q, d] = part[q, to_y, my_c] + sib_in[q, to_y]
            rows_y(q, d).start()

    def rows_own(q):
        for d in (1, 2, 3):
            rows_y(q, d).wait_recv()
        own_u[q, far] = (part[q, my_y, my_c] + sib_in[q, my_y]) + (y_in[q, 1] + y_in[q, 2] + y_in[q, 3])

    def take_own(q):
        def step(j, carry):
            put(q, j + 8, own_u[q, lax.div(j, 2), lax.rem(j, 2)])
            return carry

        lax.fori_loop(0, CL_DEV, step, 0)

    def take_halo(q):
        def step(j, carry):
            put(q, lax.rem(j + 24, 32), halo_u[q, lax.div(j, 2), lax.rem(j, 2)])
            return carry

        lax.fori_loop(0, CL_DEV, step, 0)

    def halo_pass(q):
        halo_copy(q + 1).wait_recv()
        gather_start(q + 3)

    quarter = n_rows // 4
    finish_rows(0)
    rows_sib(0).start()
    far_term(0, 1, 0, quarter)
    rows_sib(0).wait_recv()
    rows_send(0)
    far_term(0, 1, quarter, 2 * quarter)
    rows_own(0)
    halo_copy(1).start()
    gather_start(1)
    far_term(0, 1, 2 * quarter, 3 * quarter)
    gather_forward(1)
    gather_end(1)
    take_own(0)
    send_coefficients(1, 0)
    halo_pass(0)

    far_term(0, 1, 3 * quarter, n_rows)
    finish_rows(1)
    rows_sib(1).start()
    gather_forward(3)
    rows_sib(1).wait_recv()
    rows_send(1)
    gather_end(3)
    take_halo(0)
    near_term(0)
    rows_own(1)
    halo_copy(2).start()
    gather_start(2)
    far_term(1, 0, 0, quarter)
    gather_forward(2)
    gather_end(2)
    take_own(1)
    send_coefficients(1, 1)
    halo_pass(1)

    def finish_columns(q):
        def step(o, carry):
            tile = (acc[q, o] + chain[last[o]]).T
            lanes = pl.ds(pl.multiple_of(o * B, B), B)
            for j in range(4):
                part_t[q, j // 2, j % 2, :, lanes] = tile[32 * j : 32 * j + 32]
            return carry

        lax.fori_loop(0, CL_DEV, step, 0)

    def columns_sib(q):
        return remote(part_t.at[q, :, 1 - my_c], sib_t.at[q], rts_s.at[q], rts_r.at[q], me, sib)

    def columns_y(q, j):
        to_y = 2 * q + j
        d = lax.rem(to_y + FAR_Y - my_y, FAR_Y)
        return remote(mix_t.at[q, j], y_t.at[d], rty_s.at[q, j], rty_r.at[d], me, to_y * 2 + my_c)

    def columns_send(q):
        for j in range(2):
            @pl.when(my_y != 2 * q + j)
            def _():
                mix_t[q, j] = part_t[q, j, my_c] + sib_t[q, j]
                columns_y(q, j).start()

    def columns_own(q):
        for j in range(2):
            @pl.when(my_y == 2 * q + j)
            def _():
                for d in (1, 2, 3):
                    remote(mix_t.at[q, j], y_t.at[d], rty_s.at[q, j], rty_r.at[d], me, y_peer(d)).wait_recv()
                own_w[...] = (part_t[q, j, my_c] + sib_t[q, j]) + (y_t[1] + y_t[2] + y_t[3])

    far_term(1, 0, quarter, n_rows)
    finish_columns(0)
    columns_sib(0).start()
    gather_forward(4)
    columns_sib(0).wait_recv()
    columns_send(0)
    gather_end(4)
    take_halo(1)
    near_term(1)
    my_half = lax.div(my_y, 2)

    def turn(o, carry):
        lanes = pl.ds(pl.multiple_of(o * B, B), B)
        turned[0, :, lanes] = side[o, :, pl.ds(pl.multiple_of(my_half * HALF, HALF), HALF)].T
        turned[1, :, lanes] = own_u[my_half, lax.div(o, 2), lax.rem(o, 2)].T
        return carry

    lax.fori_loop(0, CL_DEV, turn, 0)
    columns_own(0)
    far_term(1, 1, 0, n_rows)
    finish_columns(1)
    columns_sib(1).start()
    columns_sib(1).wait_recv()
    columns_send(1)
    columns_own(1)

    mine = pl.ds(pl.multiple_of(lax.rem(far, 4) * 32, 32), 32)
    lane = lax.broadcasted_iota(jnp.int32, (32, B), 1)

    def dots(o, sums):
        lanes = pl.ds(pl.multiple_of(o * B, B), B)
        b, u, w = turned[0, mine, lanes], turned[1, mine, lanes], own_w[:, lanes]
        return tuple(total + item for total, item in zip(sums, (b * b, b * u, u * u, b * w, u * w, w * w)))

    sums = lax.fori_loop(0, CL_DEV, dots, tuple(jnp.zeros((32, B), F32) for _ in range(6)))
    table = jnp.zeros((32, B), F32)
    for j in range(6):
        table = jnp.where(lane == j, jnp.sum(sums[j], axis=1, keepdims=True), table)
    flat = jnp.concatenate([table, jnp.zeros((B - 32, B), F32)], axis=0).T[:8]
    gram_out[...] = flat

    def gram(k):
        return remote(gram_out, gram_in.at[k], gram_s.at[k], gram_r.at[k], ahead(k), far)

    def gram_start(k, carry):
        gram(k).start()
        return carry

    lax.fori_loop(1, n_rows, gram_start, 0)
    gram_in[0] = flat

    def gram_add(k, total):
        gram(k).wait_recv()
        return total + gram_in[k]

    total = lax.fori_loop(1, n_rows, gram_add, gram_in[0])
    weights = combine([total[j : j + 1] for j in range(6)])
    stack = jnp.concatenate(list(weights) + [jnp.zeros((B - 5, B), F32)], axis=0).T
    parts = [stack[:32, j : j + 1] for j in range(5)]
    b, u, w = turned[0, mine, :], turned[1, mine, :], own_w[...]
    sol_ref[...] = parts[0] * b + parts[1] * u
    res_ref[...] = parts[2] * b + parts[3] * u + parts[4] * w

    def settle(k, carry):
        for ap in range(2):
            for q in range(2):
                a2a(ap, q, k).wait_send()
        gram(k).wait_send()
        return carry

    lax.fori_loop(1, n_rows, settle, 0)
    for g in range(3):
        halo_copy(g).wait_send()
    for g in range(5):
        for d in range(FAR_Y):
            if d > 0:
                gather_y(g, d).wait_send()
            gather_sib(g, d).wait_send()
    for q in range(2):
        rows_sib(q).wait_send()
        columns_sib(q).wait_send()
        for d in (1, 2, 3):
            rows_y(q, d).wait_send()
        for j in range(2):
            @pl.when(my_y != 2 * q + j)
            def _():
                columns_y(q, j).wait_send()


def solution(mesh):
    n_rows = mesh.shape["rows"]
    dma = pltpu.SemaphoreType.DMA

    def shards(right_side, near_blocks, near_cols, far_src, far_tgt, far_left, far_right):
        anywhere = pl.BlockSpec(memory_space=pl.ANY)
        scalars = pl.BlockSpec(memory_space=pltpu.SMEM)
        vector = pl.BlockSpec(memory_space=pltpu.VMEM)
        sol, res = pl.pallas_call(
            functools.partial(kernel, n_rows),
            out_shape=(jax.ShapeDtypeStruct((32, CL_DEV * B), F32),) * 2,
            in_specs=[scalars] * 3 + [anywhere] * 4,
            out_specs=(vector, vector),
            scratch_shapes=[
                pltpu.VMEM((CL_DEV, B, 2 * HALF), F32),
                pltpu.VMEM((CL_DEV, NEAR_DEV, B, B), F32),
                pltpu.VMEM((CL_DEV, 2 * B, NEAR_DEV * B), BF16),
                pltpu.VMEM((n_rows, R, B), F32),
                pltpu.VMEM((n_rows, 2 * B, R), BF16),
                pltpu.VMEM((n_rows, R, B), F32),
                pltpu.VMEM((n_rows, 2 * R, B), BF16),
                pltpu.VMEM((2, 32, B, 2 * HALF), BF16),
                pltpu.VMEM((2, 2, n_rows, R, HALF), F32),
                pltpu.VMEM((2, 2, n_rows, R, HALF), F32),
                pltpu.VMEM((8, 2, B, 2 * HALF), F32),
                pltpu.VMEM((2, 8, 2, B, HALF), F32),
                pltpu.VMEM((2, 8, 2, B, HALF), F32),
                pltpu.VMEM((2, CL_DEV, B, HALF), F32),
                pltpu.VMEM((n_rows + 1, B, HALF), F32),
                pltpu.VMEM((2, 4, 2, 2, B, HALF), F32),
                pltpu.VMEM((2, 2, 2, 32, CL_DEV * B), F32),
                pltpu.VMEM((2, 4, 2, B, HALF), F32),
                pltpu.VMEM((2, 4, 2, B, HALF), F32),
                pltpu.VMEM((2, 4, 2, B, HALF), F32),
                pltpu.VMEM((2, 2, 32, CL_DEV * B), F32),
                pltpu.VMEM((2, 2, 32, CL_DEV * B), F32),
                pltpu.VMEM((4, 32, CL_DEV * B), F32),
                pltpu.VMEM((2, HALF, CL_DEV * B), F32),
                pltpu.VMEM((32, CL_DEV * B), F32),
                pltpu.VMEM((8, B), F32),
                pltpu.VMEM((n_rows, 8, B), F32),
                pltpu.SMEM((n_rows,), jnp.int32),
                pltpu.SMEM((CL_DEV,), jnp.int32),
                dma((4,)), dma((2, 2, n_rows)), dma((2, 2, n_rows)), dma((3,)), dma((3,)),
                dma((5, 4)), dma((5, 4)), dma((5, 4)), dma((5, 4)),
                dma((2,)), dma((2,)), dma((2, 4)), dma((2, 4)),
                dma((2,)), dma((2,)), dma((2, 2)), dma((4,)),
                dma((n_rows,)), dma((n_rows,)),
            ],
            compiler_params=pltpu.CompilerParams(collective_id=0, has_side_effects=True, vmem_limit_bytes=60 << 20),
            name="gmres",
        )(
            near_cols.T,
            far_src.reshape(n_rows),
            far_tgt.reshape(n_rows),
            right_side.reshape(CL_DEV, B, 2 * HALF),
            near_blocks,
            jnp.swapaxes(far_left.reshape(n_rows, B, R), 1, 2),
            jnp.swapaxes(far_right.reshape(n_rows, B, R), 1, 2),
        )
        return sol.T, res.T

    return jax.shard_map(
        shards,
        mesh=mesh,
        in_specs=(
            P("rows", None),
            P("rows", "far", None, None),
            P("rows", "far"),
            P("rows", None, "far"),
            P("rows", None, "far"),
            P("rows", None, "far", None, None),
            P("rows", None, "far", None, None),
        ),
        out_specs=(P("rows", "far"), P("rows", "far")),
        check_vma=False,
    )
```

```python
import functools

import jax
import jax.numpy as jnp
from jax import lax
from jax.experimental import pallas as pl
from jax.experimental.pallas import tpu as pltpu
from jax.sharding import PartitionSpec as P

B = 128
R = 64
HALF = 128
NEAR_DEV = 6
CL_DEV = 16
ROW_X = 4
FAR_Y = 4
UNROLL = 8
ROW_HALF = 1024
EPS = 1e-06
MESH = pl.DeviceIdType.MESH
F32 = jnp.float32
BF16 = jnp.bfloat16


def split(value):
    high = value.astype(BF16)
    return high, (value - high.astype(F32)).astype(BF16)


def quadrants(value):
    rows = value.shape[0] // 2
    return (value[:rows, :HALF] + value[:rows, HALF:]) + (value[rows:, :HALF] + value[rows:, HALF:])


def interleave(value):
    lane = lax.broadcasted_iota(jnp.int32, (value.shape[0], HALF), 1)
    first, second = value[:, :HALF], value[:, HALF:]
    return jnp.where(lane < 64, first, pltpu.roll(second, 64, 1)), jnp.where(lane < 64, pltpu.roll(first, 64, 1), second)


def combine(gram):
    bb, bu, uu, bw, uw, ww = gram
    length_sq = bb + EPS
    length = jnp.sqrt(length_sq)
    unit = bb / length_sq
    gap = EPS / length_sq
    p1, q11, p2, q12, q22 = bu / length_sq, uu / length_sq, bw / length_sq, uw / length_sq, ww / length_sq
    upper_left = 0.5 * unit + p1
    alpha = p1 - 0.5 * gap
    cand_sq = jnp.maximum(q11 - 2.0 * alpha * p1 + alpha * alpha * unit, 0.0)
    lower_sq = cand_sq + EPS
    lower_left = jnp.sqrt(lower_sq)
    f_s = (p1 - alpha * unit) / lower_left
    f_ns = (p2 - alpha * p1) / lower_left
    s_s = cand_sq / lower_sq
    s_ns = (q12 - alpha * q11 - alpha * p2 + alpha * alpha * p1) / lower_sq
    ns_ns = (q22 - 2.0 * alpha * q12 + alpha * alpha * q11) / lower_sq
    top = 0.5 * f_s + f_ns
    mid = 0.5 * s_s + s_ns
    beta = s_ns - 0.5 * EPS / lower_sq
    rest_sq = ns_ns + top * top * unit + beta * beta * s_s - 2.0 * top * f_ns - 2.0 * beta * s_ns + 2.0 * top * beta * f_s
    lower_right = jnp.sqrt(jnp.maximum(rest_sq, 0.0) + EPS)
    radius_one = jnp.sqrt(upper_left * upper_left + lower_left * lower_left)
    cosine_one = upper_left / radius_one
    sine_one = lower_left / radius_one
    rotated_top = cosine_one * length
    rotated_mid = -sine_one * length
    coupled = cosine_one * top + sine_one * mid
    diagonal_two = cosine_one * mid - sine_one * top
    radius_two = jnp.sqrt(diagonal_two * diagonal_two + lower_right * lower_right)
    weight_two = diagonal_two * rotated_mid / (radius_two * radius_two)
    weight_one = (rotated_top - coupled * weight_two) / radius_one
    one = weight_one / length
    two = weight_two / (lower_left * length)
    sol_b = one - alpha * two
    return sol_b, two, 1.0 - 0.5 * sol_b, -0.5 * two - one + alpha * two, -two


def kernel(
    n_rows,
    cols_ref, src_ref, tgt_ref, side_hbm, near_hbm, left_hbm, right_hbm,
    sol_ref, res_ref,
    side, near_raw, near, left_raw, left, right_raw, right, vcat, coef_out, coef_in,
    halo_b, own_u, halo_u, acc, chain, part, part_t,
    sib_in, mix, y_in, sib_t, mix_t, y_t, turned, own_w, gram_out, gram_in,
    prev, last,
    load_sem, a2a_s, a2a_r, halo_s, halo_r, agy_s, agy_r, ags_s, ags_r,
    rss_s, rss_r, rsy_s, rsy_r, rts_s, rts_r, rty_s, rty_r, gram_s, gram_r,
):
    n_z = n_rows // ROW_X
    me = lax.axis_index("rows")
    far = lax.axis_index("far")
    my_x, my_z = lax.rem(me, ROW_X), lax.div(me, ROW_X)
    my_y, my_c = lax.div(far, 2), lax.rem(far, 2)
    sib = my_y * 2 + 1 - my_c

    def ahead(k):
        return lax.rem(my_z + lax.div(k, ROW_X), n_z) * ROW_X + lax.rem(my_x + lax.rem(k, ROW_X), ROW_X)

    def behind(k):
        return lax.rem(my_z + n_z - lax.div(k, ROW_X), n_z) * ROW_X + lax.rem(my_x + ROW_X - lax.rem(k, ROW_X), ROW_X)

    def y_peer(d):
        return lax.rem(my_y + d, FAR_Y) * 2 + my_c

    def y_from(d):
        return lax.rem(my_y + FAR_Y - d, FAR_Y) * 2 + my_c

    def remote(src, dst, send, recv, rows, to_far):
        return pltpu.make_async_remote_copy(
            src_ref=src, dst_ref=dst, send_sem=send, recv_sem=recv,
            device_id={"rows": rows, "far": to_far}, device_id_type=MESH,
        )

    loads = [
        pltpu.make_async_copy(side_hbm, side, load_sem.at[0]),
        pltpu.make_async_copy(right_hbm, right_raw, load_sem.at[1]),
        pltpu.make_async_copy(left_hbm, left_raw, load_sem.at[2]),
        pltpu.make_async_copy(near_hbm, near_raw, load_sem.at[3]),
    ]
    for load in loads:
        load.start()

    barrier = pltpu.get_barrier_semaphore()

    def greet(k, carry):
        pl.semaphore_signal(barrier, inc=1, device_id={"rows": ahead(k), "far": far}, device_id_type=MESH)
        return carry

    lax.fori_loop(1, n_rows, greet, 0)
    for d in (1, 2, 3):
        pl.semaphore_signal(barrier, inc=1, device_id={"rows": me, "far": y_peer(d)}, device_id_type=MESH)
    pl.semaphore_signal(barrier, inc=1, device_id={"rows": me, "far": sib}, device_id_type=MESH)

    loads[0].wait()

    def put(q, slot, value):
        high, low = split(value)
        vcat[q, slot, :, :HALF] = high
        vcat[q, slot, :, HALF:] = low

    def take_side(o, carry):
        for q, item in enumerate(interleave(side[o])):
            put(q, o + 8, item)
            side[o, :, q * HALF : (q + 1) * HALF] = item
        return carry

    lax.fori_loop(0, CL_DEV, take_side, 0)
    loads[1].wait()

    def take_right(t, carry):
        high, low = split(right_raw[t])
        right[t, :R, :] = high
        right[t, R:, :] = low
        return carry

    lax.fori_loop(0, n_rows, take_right, 0)
    pl.semaphore_wait(barrier, n_rows + 3)

    halo_to = lax.rem(me + n_rows - 1 + 2 * lax.div(far, 4), n_rows)

    def halo_copy(g):
        if g == 0:
            return remote(side_hbm.at[pl.ds(2 * far, 2)], halo_b.at[far], halo_s.at[0], halo_r.at[0], halo_to, far)
        return remote(own_u.at[g - 1, far], halo_u.at[g - 1, far], halo_s.at[g], halo_r.at[g], halo_to, far)

    halo_copy(0).start()

    def a2a(ap, q, k):
        return remote(coef_out.at[ap, q, k], coef_in.at[ap, q, k], a2a_s.at[ap, q, k], a2a_r.at[ap, q, k], ahead(k), far)

    def coefficient(q, t):
        return quadrants(jnp.dot(right[t], vcat[q, src_ref[t] + 8], preferred_element_type=F32))

    def send_coefficients(ap, q):
        def step(g, carry):
            for k in [g * UNROLL + j for j in range(UNROLL)]:
                coef_out[ap, q, k] = coefficient(q, ahead(k))
                a2a(ap, q, k).start()
            return carry

        lax.fori_loop(1, n_rows // UNROLL, step, 0)
        coef_in[ap, q, 0] = coefficient(q, me)
        for k in range(1, UNROLL):
            coef_out[ap, q, k] = coefficient(q, ahead(k))
            a2a(ap, q, k).start()

    send_coefficients(0, 0)
    send_coefficients(0, 1)

    def group_ref(g, who):
        if g == 0:
            return halo_b.at[who]
        if g <= 2:
            return own_u.at[g - 1, who]
        return halo_u.at[g - 3, who]

    def gather_y(g, d):
        ref = group_ref(g, far)
        return remote(ref, ref, agy_s.at[g, d], agy_r.at[g, d], me, y_peer(d))

    def gather_sib(g, d):
        ref = group_ref(g, y_from(d))
        return remote(ref, ref, ags_s.at[g, d], ags_r.at[g, d], me, sib)

    def gather_start(g):
        for d in (2, 1, 3):
            gather_y(g, d).start()
        gather_sib(g, 0).start()

    def gather_forward(g):
        for d in (1, 3, 2):
            ref = group_ref(g, y_from(d))
            remote(ref, ref, agy_s.at[g, d], agy_r.at[g, d], me, y_peer(d)).wait_recv()
            gather_sib(g, d).start()

    def gather_end(g):
        for d in range(FAR_Y):
            ref = group_ref(g, lax.rem(my_y + FAR_Y - d, FAR_Y) * 2 + 1 - my_c)
            remote(ref, ref, ags_s.at[g, d], ags_r.at[g, d], me, sib).wait_recv()

    halo_copy(0).wait_recv()
    gather_start(0)

    def tables(k, carry):
        mine = tgt_ref[behind(k)]
        found = n_rows
        for j in range(n_rows):
            same = jnp.logical_and(tgt_ref[behind(j)] == mine, j < k)
            found = jnp.where(same, j, found)
        prev[k] = found
        return carry

    lax.fori_loop(0, n_rows, tables, 0)

    def ends(o, carry):
        found = n_rows
        for j in range(n_rows):
            found = jnp.where(tgt_ref[behind(j)] == o, j, found)
        last[o] = found
        return carry

    lax.fori_loop(0, CL_DEV, ends, 0)
    chain[n_rows] = jnp.zeros((B, HALF), F32)
    loads[2].wait()

    def take_left(a, carry):
        high, low = split(left_raw[a].T)
        left[a, :B, :] = high
        left[a, B:, :] = low
        return carry

    lax.fori_loop(0, n_rows, take_left, 0)
    gather_forward(0)
    loads[3].wait()

    def take_near(o, carry):
        for s in range(NEAR_DEV):
            high, low = split(near_raw[o, s])
            near[o, :B, s * B : (s + 1) * B] = high
            near[o, B:, s * B : (s + 1) * B] = low
        return carry

    lax.fori_loop(0, CL_DEV, take_near, 0)
    gather_end(0)

    def take_halo_b(j, carry):
        who, i = lax.div(j, 2), lax.rem(j, 2)
        slot = lax.rem(j + 24, 32)
        for q, item in enumerate(interleave(halo_b[who, i])):
            put(q, slot, item)
        return carry

    lax.fori_loop(0, CL_DEV, take_halo_b, 0)
    base = me * CL_DEV - 8

    def near_term(q):
        def step(g, carry):
            for o in [g * 4 + j for j in range(4)]:
                picked = [vcat[q, jnp.clip(cols_ref[s, o] - base, 0, 31)] for s in range(NEAR_DEV)]
                acc[q, o] = quadrants(jnp.dot(near[o], jnp.concatenate(picked, axis=0), preferred_element_type=F32))
            return carry

        lax.fori_loop(0, CL_DEV // 4, step, 0)

    def far_term(ap, q, first, end):
        def step(g, carry):
            several(g)
            return carry

        def several(g, skip=0):
            ks = [g * UNROLL + j for j in range(UNROLL)]
            for k in ks[skip:]:
                a2a(ap, q, k).wait_recv()
            here = []
            for k in ks:
                both = jnp.concatenate(split(coef_in[ap, q, k]), axis=1)
                here.append(quadrants(jnp.dot(left[behind(k)], both, preferred_element_type=F32)))
            for k, item in zip(ks, here):
                chain[k] = item + chain[prev[k]]

        if first == 0:
            several(0, 1)
        lax.fori_loop(max(first // UNROLL, 1), end // UNROLL, step, 0)

    near_term(0)
    far_term(0, 0, 0, n_rows)

    def finish_rows(q):
        def step(o, carry):
            part[q, lax.div(o, 4), lax.rem(lax.div(o, 2), 2), lax.rem(o, 2)] = acc[q, o] + chain[last[o]]
            return carry

        lax.fori_loop(0, CL_DEV, step, 0)

    def rows_sib(q, d):
        to_y = lax.rem(my_y + d, FAR_Y)
        return remote(part.at[q, to_y, 1 - my_c], sib_in.at[q, d], rss_s.at[q, d], rss_r.at[q, d], me, sib)

    def rows_y(q, d):
        return remote(mix.at[q, d], y_in.at[q, d], rsy_s.at[q, d], rsy_r.at[q, d], me, y_peer(d))

    def rows_start(q):
        for d in (2, 1, 3, 0):
            rows_sib(q, d).start()

    def rows_send(q):
        for d in (2, 1, 3):
            rows_sib(q, d).wait_recv()
            mix[q, d] = part[q, lax.rem(my_y + d, FAR_Y), my_c] + sib_in[q, d]
            rows_y(q, d).start()
        rows_sib(q, 0).wait_recv()

    def rows_own(q):
        for d in (1, 2, 3):
            rows_y(q, d).wait_recv()
        own_u[q, far] = (part[q, my_y, my_c] + sib_in[q, 0]) + (y_in[q, 1] + y_in[q, 2] + y_in[q, 3])

    def take_own(q):
        def step(j, carry):
            put(q, j + 8, own_u[q, lax.div(j, 2), lax.rem(j, 2)])
            return carry

        lax.fori_loop(0, CL_DEV, step, 0)

    def take_halo(q):
        def step(j, carry):
            put(q, lax.rem(j + 24, 32), halo_u[q, lax.div(j, 2), lax.rem(j, 2)])
            return carry

        lax.fori_loop(0, CL_DEV, step, 0)

    def halo_pass(q):
        halo_copy(q + 1).wait_recv()
        gather_start(q + 3)

    finish_rows(0)
    rows_start(0)
    near_term(1)
    rows_send(0)
    rows_own(0)
    halo_copy(1).start()
    gather_start(1)
    gather_forward(1)
    gather_end(1)
    take_own(0)
    send_coefficients(1, 0)
    halo_pass(0)

    far_term(0, 1, 0, n_rows)
    finish_rows(1)
    rows_start(1)
    rows_send(1)
    gather_forward(3)
    rows_own(1)
    halo_copy(2).start()
    gather_start(2)
    gather_forward(2)
    gather_end(2)
    take_own(1)
    send_coefficients(1, 1)
    gather_end(3)
    take_halo(0)
    near_term(0)
    halo_pass(1)

    def finish_columns(q, h):
        def step(g, carry):
            for o in [h * 8 + g * 4 + j for j in range(4)]:
                tile = (acc[q, o] + chain[last[o]]).T
                lanes = pl.ds(pl.multiple_of((g * 4 + o % 4) * B, B), B)
                for j in range(4):
                    part_t[q, h, j // 2, j % 2, :, lanes] = tile[32 * j : 32 * j + 32]
            return carry

        for g in range(2):
            step(g, 0)

    def columns_sib(q, h):
        return remote(part_t.at[q, h, :, 1 - my_c], sib_t.at[q, h], rts_s.at[q, h], rts_r.at[q, h], me, sib)

    def columns_y(q, h, j):
        to_y = q + 2 * j
        d = lax.rem(to_y + FAR_Y - my_y, FAR_Y)
        return remote(mix_t.at[q, h, j], y_t.at[h, d], rty_s.at[q, h, j], rty_r.at[h, d], me, to_y * 2 + my_c)

    def columns_send(q, h):
        for j in range(2):
            @pl.when(my_y != q + 2 * j)
            def _():
                mix_t[q, h, j] = part_t[q, h, j, my_c] + sib_t[q, h, j]
                columns_y(q, h, j).start()

    def columns_own(q, h):
        for j in range(2):
            @pl.when(my_y == q + 2 * j)
            def _():
                for d in (1, 2, 3):
                    remote(mix_t.at[q, h, j], y_t.at[h, d], rty_s.at[q, h, j], rty_r.at[h, d], me, y_peer(d)).wait_recv()
                mine = (part_t[q, h, j, my_c] + sib_t[q, h, j]) + (y_t[h, 1] + y_t[h, 2] + y_t[h, 3])
                own_w[:, h * ROW_HALF : (h + 1) * ROW_HALF] = mine

    far_term(1, 0, 0, n_rows)
    for h in range(2):
        finish_columns(0, h)
        columns_sib(0, h).start()
    gather_forward(4)
    for h in range(2):
        columns_sib(0, h).wait_recv()
        columns_send(0, h)
    gather_end(4)
    take_halo(1)
    near_term(1)
    my_half = lax.rem(my_y, 2)

    def turn(o, carry):
        lanes = pl.ds(pl.multiple_of(o * B, B), B)
        turned[0, :, lanes] = side[o, :, pl.ds(pl.multiple_of(my_half * HALF, HALF), HALF)].T
        turned[1, :, lanes] = own_u[my_half, lax.div(o, 2), lax.rem(o, 2)].T
        return carry

    lax.fori_loop(0, CL_DEV, turn, 0)
    for h in range(2):
        columns_own(0, h)
    far_term(1, 1, 0, n_rows)
    for h in range(2):
        finish_columns(1, h)
        columns_sib(1, h).start()
    for h in range(2):
        columns_sib(1, h).wait_recv()
        columns_send(1, h)
    for h in range(2):
        columns_own(1, h)

    mine = pl.ds(pl.multiple_of((lax.div(my_y, 2) * 2 + my_c) * 32, 32), 32)
    lane = lax.broadcasted_iota(jnp.int32, (32, B), 1)

    def dots(o, sums):
        lanes = pl.ds(pl.multiple_of(o * B, B), B)
        b, u, w = turned[0, mine, lanes], turned[1, mine, lanes], own_w[:, lanes]
        return tuple(total + item for total, item in zip(sums, (b * b, b * u, u * u, b * w, u * w, w * w)))

    sums = lax.fori_loop(0, CL_DEV, dots, tuple(jnp.zeros((32, B), F32) for _ in range(6)))
    table = jnp.zeros((32, B), F32)
    for j in range(6):
        table = jnp.where(lane == j, jnp.sum(sums[j], axis=1, keepdims=True), table)
    flat = jnp.concatenate([table, jnp.zeros((B - 32, B), F32)], axis=0).T[:8]
    gram_out[...] = flat

    def gram(k):
        return remote(gram_out, gram_in.at[k], gram_s.at[k], gram_r.at[k], ahead(k), far)

    def gram_start(k, carry):
        gram(k).start()
        return carry

    lax.fori_loop(1, n_rows, gram_start, 0)
    gram_in[0] = flat

    def gram_add(k, total):
        gram(k).wait_recv()
        return total + gram_in[k]

    total = lax.fori_loop(1, n_rows, gram_add, gram_in[0])
    weights = combine([total[j : j + 1] for j in range(6)])
    stack = jnp.concatenate(list(weights) + [jnp.zeros((B - 5, B), F32)], axis=0).T
    parts = [stack[:32, j : j + 1] for j in range(5)]
    b, u, w = turned[0, mine, :], turned[1, mine, :], own_w[...]
    sol_ref[...] = parts[0] * b + parts[1] * u
    res_ref[...] = parts[2] * b + parts[3] * u + parts[4] * w

    def settle(k, carry):
        for ap in range(2):
            for q in range(2):
                a2a(ap, q, k).wait_send()
        gram(k).wait_send()
        return carry

    lax.fori_loop(1, n_rows, settle, 0)
    for g in range(3):
        halo_copy(g).wait_send()
    for g in range(5):
        for d in range(FAR_Y):
            if d > 0:
                gather_y(g, d).wait_send()
            gather_sib(g, d).wait_send()
    for q in range(2):
        for d in range(FAR_Y):
            rows_sib(q, d).wait_send()
        for d in (1, 2, 3):
            rows_y(q, d).wait_send()
        for h in range(2):
            columns_sib(q, h).wait_send()
            for j in range(2):
                @pl.when(my_y != q + 2 * j)
                def _():
                    columns_y(q, h, j).wait_send()


def deliver(sol_in, res_in, sol_out, res_out, sem):
    copies = [pltpu.make_async_copy(sol_in, sol_out, sem.at[0]), pltpu.make_async_copy(res_in, res_out, sem.at[1])]
    for copy in copies:
        copy.start()
    for copy in copies:
        copy.wait()


def solution(mesh):
    n_rows = mesh.shape["rows"]
    dma = pltpu.SemaphoreType.DMA

    def shards(right_side, near_blocks, near_cols, far_src, far_tgt, far_left, far_right):
        anywhere = pl.BlockSpec(memory_space=pl.ANY)
        scalars = pl.BlockSpec(memory_space=pltpu.SMEM)
        vector = pl.BlockSpec(memory_space=pltpu.VMEM)
        sol, res = pl.pallas_call(
            functools.partial(kernel, n_rows),
            out_shape=(jax.ShapeDtypeStruct((32, CL_DEV * B), F32),) * 2,
            in_specs=[scalars] * 3 + [anywhere] * 4,
            out_specs=(vector, vector),
            scratch_shapes=[
                pltpu.VMEM((CL_DEV, B, 2 * HALF), F32),
                pltpu.VMEM((CL_DEV, NEAR_DEV, B, B), F32),
                pltpu.VMEM((CL_DEV, 2 * B, NEAR_DEV * B), BF16),
                pltpu.VMEM((n_rows, R, B), F32),
                pltpu.VMEM((n_rows, 2 * B, R), BF16),
                pltpu.VMEM((n_rows, R, B), F32),
                pltpu.VMEM((n_rows, 2 * R, B), BF16),
                pltpu.VMEM((2, 32, B, 2 * HALF), BF16),
                pltpu.VMEM((2, 2, n_rows, R, HALF), F32),
                pltpu.VMEM((2, 2, n_rows, R, HALF), F32),
                pltpu.VMEM((8, 2, B, 2 * HALF), F32),
                pltpu.VMEM((2, 8, 2, B, HALF), F32),
                pltpu.VMEM((2, 8, 2, B, HALF), F32),
                pltpu.VMEM((2, CL_DEV, B, HALF), F32),
                pltpu.VMEM((n_rows + 1, B, HALF), F32),
                pltpu.VMEM((2, 4, 2, 2, B, HALF), F32),
                pltpu.VMEM((2, 2, 2, 2, 32, ROW_HALF), F32),
                pltpu.VMEM((2, 4, 2, B, HALF), F32),
                pltpu.VMEM((2, 4, 2, B, HALF), F32),
                pltpu.VMEM((2, 4, 2, B, HALF), F32),
                pltpu.VMEM((2, 2, 2, 32, ROW_HALF), F32),
                pltpu.VMEM((2, 2, 2, 32, ROW_HALF), F32),
                pltpu.VMEM((2, 4, 32, ROW_HALF), F32),
                pltpu.VMEM((2, HALF, CL_DEV * B), F32),
                pltpu.VMEM((32, CL_DEV * B), F32),
                pltpu.VMEM((8, B), F32),
                pltpu.VMEM((n_rows, 8, B), F32),
                pltpu.SMEM((n_rows,), jnp.int32),
                pltpu.SMEM((CL_DEV,), jnp.int32),
                dma((4,)), dma((2, 2, n_rows)), dma((2, 2, n_rows)), dma((3,)), dma((3,)),
                dma((5, 4)), dma((5, 4)), dma((5, 4)), dma((5, 4)),
                dma((2, 4)), dma((2, 4)), dma((2, 4)), dma((2, 4)),
                dma((2, 2)), dma((2, 2)), dma((2, 2, 2)), dma((2, 4)),
                dma((n_rows,)), dma((n_rows,)),
            ],
            compiler_params=pltpu.CompilerParams(collective_id=0, has_side_effects=True, vmem_limit_bytes=60 << 20),
            name="gmres",
        )(
            near_cols.T,
            far_src.reshape(n_rows),
            far_tgt.reshape(n_rows),
            right_side.reshape(CL_DEV, B, 2 * HALF),
            near_blocks,
            jnp.swapaxes(far_left.reshape(n_rows, B, R), 1, 2),
            jnp.swapaxes(far_right.reshape(n_rows, B, R), 1, 2),
        )
        sol, res = pl.pallas_call(
            deliver,
            out_shape=(jax.ShapeDtypeStruct((32, CL_DEV * B), F32),) * 2,
            in_specs=[anywhere] * 2,
            out_specs=(anywhere, anywhere),
            scratch_shapes=[dma((2,))],
            name="deliver",
        )(sol, res)
        return sol.T, res.T

    return jax.shard_map(
        shards,
        mesh=mesh,
        in_specs=(
            P("rows", None),
            P("rows", "far", None, None),
            P("rows", "far"),
            P("rows", None, "far"),
            P("rows", None, "far"),
            P("rows", None, "far", None, None),
            P("rows", None, "far", None, None),
        ),
        out_specs=(P("rows", "far"), P("rows", "far")),
        check_vma=False,
    )
```

```python
import functools

import jax
import jax.numpy as jnp
from jax import lax
from jax.experimental import pallas as pl
from jax.experimental.pallas import tpu as pltpu
from jax.sharding import PartitionSpec as P

B = 128
R = 64
HALF = 128
NEAR_DEV = 6
CL_DEV = 16
ROW_X = 4
FAR_Y = 4
UNROLL = 8
ROW_HALF = 1024
EPS = 1e-06
MESH = pl.DeviceIdType.MESH
F32 = jnp.float32
BF16 = jnp.bfloat16


def split(value):
    high = value.astype(BF16)
    return high, (value - high.astype(F32)).astype(BF16)


def quadrants(value):
    rows = value.shape[0] // 2
    return (value[:rows, :HALF] + value[:rows, HALF:]) + (value[rows:, :HALF] + value[rows:, HALF:])


def interleave(value):
    lane = lax.broadcasted_iota(jnp.int32, (value.shape[0], HALF), 1)
    first, second = value[:, :HALF], value[:, HALF:]
    return jnp.where(lane < 64, first, pltpu.roll(second, 64, 1)), jnp.where(lane < 64, pltpu.roll(first, 64, 1), second)


def combine(gram):
    bb, bu, uu, bw, uw, ww = gram
    length_sq = bb + EPS
    length = jnp.sqrt(length_sq)
    unit = bb / length_sq
    gap = EPS / length_sq
    p1, q11, p2, q12, q22 = bu / length_sq, uu / length_sq, bw / length_sq, uw / length_sq, ww / length_sq
    upper_left = 0.5 * unit + p1
    alpha = p1 - 0.5 * gap
    cand_sq = jnp.maximum(q11 - 2.0 * alpha * p1 + alpha * alpha * unit, 0.0)
    lower_sq = cand_sq + EPS
    lower_left = jnp.sqrt(lower_sq)
    f_s = (p1 - alpha * unit) / lower_left
    f_ns = (p2 - alpha * p1) / lower_left
    s_s = cand_sq / lower_sq
    s_ns = (q12 - alpha * q11 - alpha * p2 + alpha * alpha * p1) / lower_sq
    ns_ns = (q22 - 2.0 * alpha * q12 + alpha * alpha * q11) / lower_sq
    top = 0.5 * f_s + f_ns
    mid = 0.5 * s_s + s_ns
    beta = s_ns - 0.5 * EPS / lower_sq
    rest_sq = ns_ns + top * top * unit + beta * beta * s_s - 2.0 * top * f_ns - 2.0 * beta * s_ns + 2.0 * top * beta * f_s
    lower_right = jnp.sqrt(jnp.maximum(rest_sq, 0.0) + EPS)
    radius_one = jnp.sqrt(upper_left * upper_left + lower_left * lower_left)
    cosine_one = upper_left / radius_one
    sine_one = lower_left / radius_one
    rotated_top = cosine_one * length
    rotated_mid = -sine_one * length
    coupled = cosine_one * top + sine_one * mid
    diagonal_two = cosine_one * mid - sine_one * top
    radius_two = jnp.sqrt(diagonal_two * diagonal_two + lower_right * lower_right)
    weight_two = diagonal_two * rotated_mid / (radius_two * radius_two)
    weight_one = (rotated_top - coupled * weight_two) / radius_one
    one = weight_one / length
    two = weight_two / (lower_left * length)
    sol_b = one - alpha * two
    return sol_b, two, 1.0 - 0.5 * sol_b, -0.5 * two - one + alpha * two, -two


def kernel(
    n_rows,
    cols_ref, src_ref, tgt_ref, side_hbm, near_hbm, left_hbm, right_hbm,
    sol_ref, res_ref,
    side, near_raw, near, left_raw, left, right_raw, right, vcat, coef_out, coef_in,
    halo_b, own_u, halo_u, acc, chain, part, part_t,
    sib_in, mix, y_in, sib_t, mix_t, y_t, turned, own_w, gram_out, gram_in,
    prev, last,
    load_sem, a2a_s, a2a_r, halo_s, halo_r, agy_s, agy_r, ags_s, ags_r,
    rss_s, rss_r, rsy_s, rsy_r, rts_s, rts_r, rty_s, rty_r, gram_s, gram_r,
):
    n_z = n_rows // ROW_X
    me = lax.axis_index("rows")
    far = lax.axis_index("far")
    my_x, my_z = lax.rem(me, ROW_X), lax.div(me, ROW_X)
    my_y, my_c = lax.div(far, 2), lax.rem(far, 2)
    sib = my_y * 2 + 1 - my_c

    def ahead(k):
        return lax.rem(my_z + lax.div(k, ROW_X), n_z) * ROW_X + lax.rem(my_x + lax.rem(k, ROW_X), ROW_X)

    def behind(k):
        return lax.rem(my_z + n_z - lax.div(k, ROW_X), n_z) * ROW_X + lax.rem(my_x + ROW_X - lax.rem(k, ROW_X), ROW_X)

    def y_peer(d):
        return lax.rem(my_y + d, FAR_Y) * 2 + my_c

    def y_from(d):
        return lax.rem(my_y + FAR_Y - d, FAR_Y) * 2 + my_c

    def remote(src, dst, send, recv, rows, to_far):
        return pltpu.make_async_remote_copy(
            src_ref=src, dst_ref=dst, send_sem=send, recv_sem=recv,
            device_id={"rows": rows, "far": to_far}, device_id_type=MESH,
        )

    loads = [
        pltpu.make_async_copy(side_hbm, side, load_sem.at[0]),
        pltpu.make_async_copy(right_hbm, right_raw, load_sem.at[1]),
        pltpu.make_async_copy(left_hbm, left_raw, load_sem.at[2]),
        pltpu.make_async_copy(near_hbm, near_raw, load_sem.at[3]),
    ]
    for load in loads:
        load.start()

    barrier = pltpu.get_barrier_semaphore()

    def greet(k, carry):
        pl.semaphore_signal(barrier, inc=1, device_id={"rows": ahead(k), "far": far}, device_id_type=MESH)
        return carry

    lax.fori_loop(1, n_rows, greet, 0)
    for d in (1, 2, 3):
        pl.semaphore_signal(barrier, inc=1, device_id={"rows": me, "far": y_peer(d)}, device_id_type=MESH)
    pl.semaphore_signal(barrier, inc=1, device_id={"rows": me, "far": sib}, device_id_type=MESH)

    loads[0].wait()

    def put(q, slot, value):
        high, low = split(value)
        vcat[q, slot, :, :HALF] = high
        vcat[q, slot, :, HALF:] = low

    def take_side(o, carry):
        for q, item in enumerate(interleave(side[o])):
            put(q, o + 8, item)
            side[o, :, q * HALF : (q + 1) * HALF] = item
        return carry

    lax.fori_loop(0, CL_DEV, take_side, 0)
    loads[1].wait()

    def take_right(t, carry):
        high, low = split(right_raw[t])
        right[t, :R, :] = high
        right[t, R:, :] = low
        return carry

    lax.fori_loop(0, n_rows, take_right, 0)
    pl.semaphore_wait(barrier, n_rows + 3)

    halo_to = lax.rem(me + n_rows - 1 + 2 * lax.div(far, 4), n_rows)

    def halo_copy(g):
        if g >= 3:
            rows = side.at[pl.ds(2 * far, 2), :, pl.ds((g - 3) * HALF, HALF)]
            return remote(rows, halo_b.at[g - 3, far], halo_s.at[g], halo_r.at[g], halo_to, far)
        return remote(own_u.at[g - 1, far], halo_u.at[g - 1, far], halo_s.at[g], halo_r.at[g], halo_to, far)

    halo_copy(3).start()
    halo_copy(4).start()

    def a2a(ap, q, k):
        return remote(coef_out.at[ap, q, k], coef_in.at[ap, q, k], a2a_s.at[ap, q, k], a2a_r.at[ap, q, k], ahead(k), far)

    def settle(ap, q, k):
        a2a(ap, q, k).wait_send()
        return 0

    def coefficient(q, t):
        return quadrants(jnp.dot(right[t], vcat[q, src_ref[t] + 8], preferred_element_type=F32))

    def send_coefficients(ap, q):
        def step(g, carry):
            for k in [g * UNROLL + j for j in range(UNROLL)]:
                coef_out[ap, q, k] = coefficient(q, ahead(k))
                a2a(ap, q, k).start()
            return carry

        lax.fori_loop(1, n_rows // UNROLL, step, 0)
        coef_in[ap, q, 0] = coefficient(q, me)
        for k in range(1, UNROLL):
            coef_out[ap, q, k] = coefficient(q, ahead(k))
            a2a(ap, q, k).start()

    send_coefficients(0, 0)
    send_coefficients(0, 1)

    def group_ref(g, who):
        if g in (0, 5):
            return halo_b.at[g // 5, who]
        if g <= 2:
            return own_u.at[g - 1, who]
        return halo_u.at[g - 3, who]

    def gather_y(g, d):
        ref = group_ref(g, far)
        return remote(ref, ref, agy_s.at[g, d], agy_r.at[g, d], me, y_peer(d))

    def gather_sib(g, d):
        ref = group_ref(g, y_from(d))
        return remote(ref, ref, ags_s.at[g, d], ags_r.at[g, d], me, sib)

    def gather_start(g):
        for d in (2, 1, 3):
            gather_y(g, d).start()
        gather_sib(g, 0).start()

    def gather_forward(g):
        for d in (1, 3, 2):
            ref = group_ref(g, y_from(d))
            remote(ref, ref, agy_s.at[g, d], agy_r.at[g, d], me, y_peer(d)).wait_recv()
            gather_sib(g, d).start()

    def gather_end(g):
        for d in range(FAR_Y):
            ref = group_ref(g, lax.rem(my_y + FAR_Y - d, FAR_Y) * 2 + 1 - my_c)
            remote(ref, ref, ags_s.at[g, d], ags_r.at[g, d], me, sib).wait_recv()

    for q in range(2):
        halo_copy(q + 3).wait_recv()
        gather_start(q * 5)

    def tables(k, carry):
        mine = tgt_ref[behind(k)]
        found = n_rows
        for j in range(n_rows):
            same = jnp.logical_and(tgt_ref[behind(j)] == mine, j < k)
            found = jnp.where(same, j, found)
        prev[k] = found
        return carry

    lax.fori_loop(0, n_rows, tables, 0)

    def ends(o, carry):
        found = n_rows
        for j in range(n_rows):
            found = jnp.where(tgt_ref[behind(j)] == o, j, found)
        last[o] = found
        return carry

    lax.fori_loop(0, CL_DEV, ends, 0)
    chain[n_rows] = jnp.zeros((B, HALF), F32)
    loads[2].wait()

    def take_left(a, carry):
        high, low = split(left_raw[a].T)
        left[a, :B, :] = high
        left[a, B:, :] = low
        return carry

    lax.fori_loop(0, n_rows, take_left, 0)
    gather_forward(0)
    loads[3].wait()

    def take_near(o, carry):
        for s in range(NEAR_DEV):
            high, low = split(near_raw[o, s])
            near[o, :B, s * B : (s + 1) * B] = high
            near[o, B:, s * B : (s + 1) * B] = low
        return carry

    lax.fori_loop(0, CL_DEV, take_near, 0)

    def take_halo(q, halo):
        def step(j, carry):
            put(q, lax.rem(j + 24, 32), halo[q, lax.div(j, 2), lax.rem(j, 2)])
            return carry

        lax.fori_loop(0, CL_DEV, step, 0)

    gather_end(0)
    take_halo(0, halo_b)
    base = me * CL_DEV - 8

    def near_term(q):
        def step(g, carry):
            for o in [g * 4 + j for j in range(4)]:
                picked = [vcat[q, jnp.clip(cols_ref[s, o] - base, 0, 31)] for s in range(NEAR_DEV)]
                acc[q, o] = quadrants(jnp.dot(near[o], jnp.concatenate(picked, axis=0), preferred_element_type=F32))
            return carry

        lax.fori_loop(0, CL_DEV // 4, step, 0)

    def far_term(ap, q, first, end):
        def step(g, carry):
            several(g)
            return carry

        def several(g, skip=0):
            ks = [g * UNROLL + j for j in range(UNROLL)]
            for k in ks[skip:]:
                a2a(ap, q, k).wait_recv()
            here = []
            for k in ks:
                both = jnp.concatenate(split(coef_in[ap, q, k]), axis=1)
                here.append(quadrants(jnp.dot(left[behind(k)], both, preferred_element_type=F32)))
            for k, item in zip(ks, here):
                chain[k] = item + chain[prev[k]]

        if first == 0:
            several(0, 1)
        lax.fori_loop(max(first // UNROLL, 1), end // UNROLL, step, 0)

    near_term(0)
    far_term(0, 0, 0, n_rows)

    def finish_rows(q):
        def step(o, carry):
            part[q, lax.div(o, 4), lax.rem(lax.div(o, 2), 2), lax.rem(o, 2)] = acc[q, o] + chain[last[o]]
            return carry

        lax.fori_loop(0, CL_DEV, step, 0)

    def rows_sib(q, d):
        to_y = lax.rem(my_y + d, FAR_Y)
        return remote(part.at[q, to_y, 1 - my_c], sib_in.at[q, d], rss_s.at[q, d], rss_r.at[q, d], me, sib)

    def rows_y(q, d):
        return remote(mix.at[q, d], y_in.at[q, d], rsy_s.at[q, d], rsy_r.at[q, d], me, y_peer(d))

    def rows_start(q):
        for d in (2, 1, 3, 0):
            rows_sib(q, d).start()

    def rows_send(q):
        for d in (2, 1, 3):
            rows_sib(q, d).wait_recv()
            mix[q, d] = part[q, lax.rem(my_y + d, FAR_Y), my_c] + sib_in[q, d]
            rows_y(q, d).start()
        rows_sib(q, 0).wait_recv()

    def rows_own(q):
        for d in (1, 2, 3):
            rows_y(q, d).wait_recv()
        own_u[q, far] = (part[q, my_y, my_c] + sib_in[q, 0]) + (y_in[q, 1] + y_in[q, 2] + y_in[q, 3])

    def take_own(q):
        def step(j, carry):
            put(q, j + 8, own_u[q, lax.div(j, 2), lax.rem(j, 2)])
            return carry

        lax.fori_loop(0, CL_DEV, step, 0)

    finish_rows(0)
    rows_start(0)
    rows_send(0)
    gather_forward(5)
    gather_end(5)
    take_halo(1, halo_b)
    near_term(1)
    rows_own(0)
    halo_copy(1).start()
    gather_start(1)
    gather_forward(1)
    gather_end(1)
    take_own(0)
    send_coefficients(1, 0)

    far_term(0, 1, 0, n_rows)
    finish_rows(1)
    rows_start(1)
    rows_send(1)
    halo_copy(1).wait_recv()
    rows_own(1)
    halo_copy(2).start()
    gather_start(2)
    gather_start(3)
    gather_forward(2)
    gather_end(2)
    take_own(1)
    send_coefficients(1, 1)
    gather_forward(3)
    halo_copy(2).wait_recv()
    gather_start(4)
    gather_end(3)
    take_halo(0, halo_u)
    near_term(0)

    def finish_columns(q, h):
        def step(g, carry):
            for o in [h * 8 + g * 4 + j for j in range(4)]:
                tile = (acc[q, o] + chain[last[o]]).T
                lanes = pl.ds(pl.multiple_of((g * 4 + o % 4) * B, B), B)
                for j in range(4):
                    part_t[q, h, j // 2, j % 2, :, lanes] = tile[32 * j : 32 * j + 32]
            return carry

        for g in range(2):
            step(g, 0)

    def columns_sib(q, h):
        return remote(part_t.at[q, h, :, 1 - my_c], sib_t.at[q, h], rts_s.at[q, h], rts_r.at[q, h], me, sib)

    def columns_y(q, h, j):
        to_y = q + 2 * j
        d = lax.rem(to_y + FAR_Y - my_y, FAR_Y)
        return remote(mix_t.at[q, h, j], y_t.at[h, d], rty_s.at[q, h, j], rty_r.at[h, d], me, to_y * 2 + my_c)

    def columns_send(q, h):
        for j in range(2):
            @pl.when(my_y != q + 2 * j)
            def _():
                mix_t[q, h, j] = part_t[q, h, j, my_c] + sib_t[q, h, j]
                columns_y(q, h, j).start()

    def columns_own(q, h):
        for j in range(2):
            @pl.when(my_y == q + 2 * j)
            def _():
                for d in (1, 2, 3):
                    remote(mix_t.at[q, h, j], y_t.at[h, d], rty_s.at[q, h, j], rty_r.at[h, d], me, y_peer(d)).wait_recv()
                mine = (part_t[q, h, j, my_c] + sib_t[q, h, j]) + (y_t[h, 1] + y_t[h, 2] + y_t[h, 3])
                own_w[:, h * ROW_HALF : (h + 1) * ROW_HALF] = mine

    far_term(1, 0, 0, n_rows)
    for h in range(2):
        finish_columns(0, h)
        columns_sib(0, h).start()
    gather_forward(4)
    for h in range(2):
        columns_sib(0, h).wait_recv()
        columns_send(0, h)
    gather_end(4)
    take_halo(1, halo_u)
    near_term(1)
    my_half = lax.rem(my_y, 2)

    def turn(o, carry):
        lanes = pl.ds(pl.multiple_of(o * B, B), B)
        turned[0, :, lanes] = side[o, :, pl.ds(pl.multiple_of(my_half * HALF, HALF), HALF)].T
        turned[1, :, lanes] = own_u[my_half, lax.div(o, 2), lax.rem(o, 2)].T
        return carry

    lax.fori_loop(0, CL_DEV, turn, 0)
    for h in range(2):
        columns_own(0, h)
    mine = pl.ds(pl.multiple_of((lax.div(my_y, 2) * 2 + my_c) * 32, 32), 32)
    lane = lax.broadcasted_iota(jnp.int32, (32, B), 1)

    def dots(pairs):
        def step(o, sums):
            lanes = pl.ds(pl.multiple_of(o * B, B), B)
            items = (turned[0, mine, lanes], turned[1, mine, lanes], own_w[:, lanes] if pairs[-1][1] == 2 else None)
            return tuple(total + items[i] * items[j] for total, (i, j) in zip(sums, pairs))

        sums = lax.fori_loop(0, CL_DEV, step, tuple(jnp.zeros((32, B), F32) for _ in pairs))
        return [jnp.sum(item, axis=1, keepdims=True) for item in sums]

    early = dots(((0, 0), (0, 1), (1, 1)))
    for q in range(2):
        lax.fori_loop(1, n_rows, lambda k, carry: settle(0, q, k), 0)
    far_term(1, 1, 0, n_rows)
    for h in range(2):
        finish_columns(1, h)
        columns_sib(1, h).start()
    for h in range(2):
        columns_sib(1, h).wait_recv()
        columns_send(1, h)
    for q in range(2):
        lax.fori_loop(1, n_rows, lambda k, carry: settle(1, q, k), 0)
    for h in range(2):
        columns_own(1, h)

    table = jnp.zeros((32, B), F32)
    for j, item in enumerate(early + dots(((0, 2), (1, 2), (2, 2)))):
        table = jnp.where(lane == j, item, table)
    flat = jnp.concatenate([table, jnp.zeros((B - 32, B), F32)], axis=0).T[:8]
    gram_out[...] = flat

    def gram(k):
        return remote(gram_out, gram_in.at[k], gram_s.at[k], gram_r.at[k], ahead(k), far)

    def gram_start(k, carry):
        gram(k).start()
        return carry

    def gram_settle(k, carry):
        gram(k).wait_send()
        return carry

    lax.fori_loop(1, n_rows, gram_start, 0)
    gram_in[0] = flat

    def gram_add(k, total):
        gram(k).wait_recv()
        return total + gram_in[k]

    total = lax.fori_loop(1, n_rows, gram_add, gram_in[0])
    weights = combine([total[j : j + 1] for j in range(6)])
    stack = jnp.concatenate(list(weights) + [jnp.zeros((B - 5, B), F32)], axis=0).T
    parts = [stack[:32, j : j + 1] for j in range(5)]
    b, u, w = turned[0, mine, :], turned[1, mine, :], own_w[...]
    sol_ref[...] = parts[0] * b + parts[1] * u
    res_ref[...] = parts[2] * b + parts[3] * u + parts[4] * w

    lax.fori_loop(1, n_rows, gram_settle, 0)
    for g in (1, 2, 3, 4):
        halo_copy(g).wait_send()
    for g in range(6):
        for d in range(FAR_Y):
            if d > 0:
                gather_y(g, d).wait_send()
            gather_sib(g, d).wait_send()
    for q in range(2):
        for d in range(FAR_Y):
            rows_sib(q, d).wait_send()
        for d in (1, 2, 3):
            rows_y(q, d).wait_send()
        for h in range(2):
            columns_sib(q, h).wait_send()
            for j in range(2):
                @pl.when(my_y != q + 2 * j)
                def _():
                    columns_y(q, h, j).wait_send()


def deliver(sol_in, res_in, sol_out, res_out):
    sol_out[...] = sol_in[...]
    res_out[...] = res_in[...]


def solution(mesh):
    n_rows = mesh.shape["rows"]
    dma = pltpu.SemaphoreType.DMA

    def shards(right_side, near_blocks, near_cols, far_src, far_tgt, far_left, far_right):
        anywhere = pl.BlockSpec(memory_space=pl.ANY)
        scalars = pl.BlockSpec(memory_space=pltpu.SMEM)
        vector = pl.BlockSpec(memory_space=pltpu.VMEM)
        sol, res = pl.pallas_call(
            functools.partial(kernel, n_rows),
            out_shape=(jax.ShapeDtypeStruct((32, CL_DEV * B), F32),) * 2,
            in_specs=[scalars] * 3 + [anywhere] * 4,
            out_specs=(vector, vector),
            scratch_shapes=[
                pltpu.VMEM((CL_DEV, B, 2 * HALF), F32),
                pltpu.VMEM((CL_DEV, NEAR_DEV, B, B), F32),
                pltpu.VMEM((CL_DEV, 2 * B, NEAR_DEV * B), BF16),
                pltpu.VMEM((n_rows, R, B), F32),
                pltpu.VMEM((n_rows, 2 * B, R), BF16),
                pltpu.VMEM((n_rows, R, B), F32),
                pltpu.VMEM((n_rows, 2 * R, B), BF16),
                pltpu.VMEM((2, 32, B, 2 * HALF), BF16),
                pltpu.VMEM((2, 2, n_rows, R, HALF), F32),
                pltpu.VMEM((2, 2, n_rows, R, HALF), F32),
                pltpu.VMEM((2, 8, 2, B, HALF), F32),
                pltpu.VMEM((2, 8, 2, B, HALF), F32),
                pltpu.VMEM((2, 8, 2, B, HALF), F32),
                pltpu.VMEM((2, CL_DEV, B, HALF), F32),
                pltpu.VMEM((n_rows + 1, B, HALF), F32),
                pltpu.VMEM((2, 4, 2, 2, B, HALF), F32),
                pltpu.VMEM((2, 2, 2, 2, 32, ROW_HALF), F32),
                pltpu.VMEM((2, 4, 2, B, HALF), F32),
                pltpu.VMEM((2, 4, 2, B, HALF), F32),
                pltpu.VMEM((2, 4, 2, B, HALF), F32),
                pltpu.VMEM((2, 2, 2, 32, ROW_HALF), F32),
                pltpu.VMEM((2, 2, 2, 32, ROW_HALF), F32),
                pltpu.VMEM((2, 4, 32, ROW_HALF), F32),
                pltpu.VMEM((2, HALF, CL_DEV * B), F32),
                pltpu.VMEM((32, CL_DEV * B), F32),
                pltpu.VMEM((8, B), F32),
                pltpu.VMEM((n_rows, 8, B), F32),
                pltpu.SMEM((n_rows,), jnp.int32),
                pltpu.SMEM((CL_DEV,), jnp.int32),
                dma((4,)), dma((2, 2, n_rows)), dma((2, 2, n_rows)), dma((5,)), dma((5,)),
                dma((6, 4)), dma((6, 4)), dma((6, 4)), dma((6, 4)),
                dma((2, 4)), dma((2, 4)), dma((2, 4)), dma((2, 4)),
                dma((2, 2)), dma((2, 2)), dma((2, 2, 2)), dma((2, 4)),
                dma((n_rows,)), dma((n_rows,)),
            ],
            compiler_params=pltpu.CompilerParams(collective_id=0, has_side_effects=True, vmem_limit_bytes=60 << 20),
            name="gmres",
        )(
            near_cols.T,
            far_src.reshape(n_rows),
            far_tgt.reshape(n_rows),
            right_side.reshape(CL_DEV, B, 2 * HALF),
            near_blocks,
            jnp.swapaxes(far_left.reshape(n_rows, B, R), 1, 2),
            jnp.swapaxes(far_right.reshape(n_rows, B, R), 1, 2),
        )
        sol, res = pl.pallas_call(
            deliver,
            out_shape=(jax.ShapeDtypeStruct((32, CL_DEV * B), F32),) * 2,
            in_specs=[vector] * 2,
            out_specs=(vector, vector),
            name="deliver",
        )(sol, res)
        return sol.T, res.T

    return jax.shard_map(
        shards,
        mesh=mesh,
        in_specs=(
            P("rows", None),
            P("rows", "far", None, None),
            P("rows", "far"),
            P("rows", None, "far"),
            P("rows", None, "far"),
            P("rows", None, "far", None, None),
            P("rows", None, "far", None, None),
        ),
        out_specs=(P("rows", "far"), P("rows", "far")),
        check_vma=False,
    )
```

```python
import functools

import jax
import jax.numpy as jnp
from jax import lax
from jax.experimental import pallas as pl
from jax.experimental.pallas import tpu as pltpu
from jax.sharding import PartitionSpec as P

B = 128
R = 64
HALF = 128
NEAR_DEV = 6
CL_DEV = 16
ROW_X = 4
FAR_Y = 4
UNROLL = 8
ROW_HALF = 1024
EPS = 1e-06
MESH = pl.DeviceIdType.MESH
F32 = jnp.float32
BF16 = jnp.bfloat16


def split(value):
    high = value.astype(BF16)
    return high, (value - high.astype(F32)).astype(BF16)


def quadrants(value):
    rows = value.shape[0] // 2
    return (value[:rows, :HALF] + value[:rows, HALF:]) + (value[rows:, :HALF] + value[rows:, HALF:])


def interleave(value):
    lane = lax.broadcasted_iota(jnp.int32, (value.shape[0], HALF), 1)
    first, second = value[:, :HALF], value[:, HALF:]
    return jnp.where(lane < 64, first, pltpu.roll(second, 64, 1)), jnp.where(lane < 64, pltpu.roll(first, 64, 1), second)


def combine(gram):
    bb, bu, uu, bw, uw, ww = gram
    length_sq = bb + EPS
    length = jnp.sqrt(length_sq)
    unit = bb / length_sq
    gap = EPS / length_sq
    p1, q11, p2, q12, q22 = bu / length_sq, uu / length_sq, bw / length_sq, uw / length_sq, ww / length_sq
    upper_left = 0.5 * unit + p1
    alpha = p1 - 0.5 * gap
    cand_sq = jnp.maximum(q11 - 2.0 * alpha * p1 + alpha * alpha * unit, 0.0)
    lower_sq = cand_sq + EPS
    lower_left = jnp.sqrt(lower_sq)
    f_s = (p1 - alpha * unit) / lower_left
    f_ns = (p2 - alpha * p1) / lower_left
    s_s = cand_sq / lower_sq
    s_ns = (q12 - alpha * q11 - alpha * p2 + alpha * alpha * p1) / lower_sq
    ns_ns = (q22 - 2.0 * alpha * q12 + alpha * alpha * q11) / lower_sq
    top = 0.5 * f_s + f_ns
    mid = 0.5 * s_s + s_ns
    beta = s_ns - 0.5 * EPS / lower_sq
    rest_sq = ns_ns + top * top * unit + beta * beta * s_s - 2.0 * top * f_ns - 2.0 * beta * s_ns + 2.0 * top * beta * f_s
    lower_right = jnp.sqrt(jnp.maximum(rest_sq, 0.0) + EPS)
    radius_one = jnp.sqrt(upper_left * upper_left + lower_left * lower_left)
    cosine_one = upper_left / radius_one
    sine_one = lower_left / radius_one
    rotated_top = cosine_one * length
    rotated_mid = -sine_one * length
    coupled = cosine_one * top + sine_one * mid
    diagonal_two = cosine_one * mid - sine_one * top
    radius_two = jnp.sqrt(diagonal_two * diagonal_two + lower_right * lower_right)
    weight_two = diagonal_two * rotated_mid / (radius_two * radius_two)
    weight_one = (rotated_top - coupled * weight_two) / radius_one
    one = weight_one / length
    two = weight_two / (lower_left * length)
    sol_b = one - alpha * two
    return sol_b, two, 1.0 - 0.5 * sol_b, -0.5 * two - one + alpha * two, -two


def kernel(
    n_rows,
    cols_ref, src_ref, tgt_ref, side_hbm, near_hbm, left_hbm, right_hbm,
    sol_ref, res_ref,
    side, near_raw, near, left_raw, left, right_raw, right, vcat, coef_out, coef_in,
    halo_b, own_u, halo_u, acc, chain, part, part_t,
    sib_in, mix, y_in, sib_t, mix_t, y_t, turned, own_w, gram_out, gram_in,
    prev, last,
    load_sem, a2a_s, a2a_r, halo_s, halo_r, agy_s, agy_r, ags_s, ags_r,
    rss_s, rss_r, rsy_s, rsy_r, rts_s, rts_r, rty_s, rty_r, gram_s, gram_r,
):
    n_z = n_rows // ROW_X
    me = lax.axis_index("rows")
    far = lax.axis_index("far")
    my_x, my_z = lax.rem(me, ROW_X), lax.div(me, ROW_X)
    my_y, my_c = lax.div(far, 2), lax.rem(far, 2)
    sib = my_y * 2 + 1 - my_c

    def ahead(k):
        return lax.rem(my_z + lax.div(k, ROW_X), n_z) * ROW_X + lax.rem(my_x + lax.rem(k, ROW_X), ROW_X)

    def behind(k):
        return lax.rem(my_z + n_z - lax.div(k, ROW_X), n_z) * ROW_X + lax.rem(my_x + ROW_X - lax.rem(k, ROW_X), ROW_X)

    def y_peer(d):
        return lax.rem(my_y + d, FAR_Y) * 2 + my_c

    def y_from(d):
        return lax.rem(my_y + FAR_Y - d, FAR_Y) * 2 + my_c

    def remote(src, dst, send, recv, rows, to_far):
        return pltpu.make_async_remote_copy(
            src_ref=src, dst_ref=dst, send_sem=send, recv_sem=recv,
            device_id={"rows": rows, "far": to_far}, device_id_type=MESH,
        )

    loads = [
        pltpu.make_async_copy(side_hbm, side, load_sem.at[0]),
        pltpu.make_async_copy(right_hbm, right_raw, load_sem.at[1]),
        pltpu.make_async_copy(left_hbm, left_raw, load_sem.at[2]),
        pltpu.make_async_copy(near_hbm, near_raw, load_sem.at[3]),
    ]
    for load in loads:
        load.start()

    barrier = pltpu.get_barrier_semaphore()

    def greet(k, carry):
        pl.semaphore_signal(barrier, inc=1, device_id={"rows": ahead(k), "far": far}, device_id_type=MESH)
        return carry

    lax.fori_loop(1, n_rows, greet, 0)
    for d in (1, 2, 3):
        pl.semaphore_signal(barrier, inc=1, device_id={"rows": me, "far": y_peer(d)}, device_id_type=MESH)
    pl.semaphore_signal(barrier, inc=1, device_id={"rows": me, "far": sib}, device_id_type=MESH)

    loads[0].wait()

    def put(q, slot, value):
        high, low = split(value)
        vcat[q, slot, :, :HALF] = high
        vcat[q, slot, :, HALF:] = low

    def take_side(o, carry):
        for q, item in enumerate(interleave(side[o])):
            put(q, o + 8, item)
            side[o, :, q * HALF : (q + 1) * HALF] = item
        return carry

    lax.fori_loop(0, CL_DEV, take_side, 0)
    loads[1].wait()

    def take_right(t, carry):
        high, low = split(right_raw[t])
        right[t, :R, :] = high
        right[t, R:, :] = low
        return carry

    lax.fori_loop(0, n_rows, take_right, 0)
    pl.semaphore_wait(barrier, n_rows + 3)

    halo_to = lax.rem(me + n_rows - 1 + 2 * lax.div(far, 4), n_rows)

    def halo_copy(g):
        if g >= 3:
            rows = side.at[pl.ds(2 * far, 2), :, pl.ds((g - 3) * HALF, HALF)]
            return remote(rows, halo_b.at[g - 3, far], halo_s.at[g], halo_r.at[g], halo_to, far)
        return remote(own_u.at[g - 1, far], halo_u.at[g - 1, far], halo_s.at[g], halo_r.at[g], halo_to, far)

    halo_copy(3).start()
    halo_copy(4).start()

    def a2a(ap, q, k):
        return remote(coef_out.at[ap, q, k], coef_in.at[ap, q, k], a2a_s.at[ap, q, k], a2a_r.at[ap, q, k], ahead(k), far)

    def settle(ap, q, k):
        a2a(ap, q, k).wait_send()
        return 0

    def coefficient(q, t):
        return quadrants(jnp.dot(right[t], vcat[q, src_ref[t] + 8], preferred_element_type=F32))

    def send_coefficients(ap, q):
        def step(g, carry):
            for k in [g * UNROLL + j for j in range(UNROLL)]:
                coef_out[ap, q, k] = coefficient(q, ahead(k))
                a2a(ap, q, k).start()
            return carry

        lax.fori_loop(1, n_rows // UNROLL, step, 0)
        coef_in[ap, q, 0] = coefficient(q, me)
        for k in range(1, UNROLL):
            coef_out[ap, q, k] = coefficient(q, ahead(k))
            a2a(ap, q, k).start()

    send_coefficients(0, 0)
    send_coefficients(0, 1)

    def group_ref(g, who):
        if g in (0, 5):
            return halo_b.at[g // 5, who]
        if g <= 2:
            return own_u.at[g - 1, who]
        return halo_u.at[g - 3, who]

    def gather_y(g, d):
        ref = group_ref(g, far)
        return remote(ref, ref, agy_s.at[g, d], agy_r.at[g, d], me, y_peer(d))

    def gather_sib(g, d):
        ref = group_ref(g, y_from(d))
        return remote(ref, ref, ags_s.at[g, d], ags_r.at[g, d], me, sib)

    def gather_start(g):
        for d in (2, 1, 3):
            gather_y(g, d).start()
        gather_sib(g, 0).start()

    def gather_forward(g):
        for d in (1, 3, 2):
            ref = group_ref(g, y_from(d))
            remote(ref, ref, agy_s.at[g, d], agy_r.at[g, d], me, y_peer(d)).wait_recv()
            gather_sib(g, d).start()

    def gather_end(g):
        for d in range(FAR_Y):
            ref = group_ref(g, lax.rem(my_y + FAR_Y - d, FAR_Y) * 2 + 1 - my_c)
            remote(ref, ref, ags_s.at[g, d], ags_r.at[g, d], me, sib).wait_recv()

    for q in range(2):
        halo_copy(q + 3).wait_recv()
        gather_start(q * 5)

    def tables(k, carry):
        mine = tgt_ref[behind(k)]
        found = n_rows
        for j in range(n_rows):
            same = jnp.logical_and(tgt_ref[behind(j)] == mine, j < k)
            found = jnp.where(same, j, found)
        prev[k] = found
        return carry

    lax.fori_loop(0, n_rows, tables, 0)

    def ends(o, carry):
        found = n_rows
        for j in range(n_rows):
            found = jnp.where(tgt_ref[behind(j)] == o, j, found)
        last[o] = found
        return carry

    lax.fori_loop(0, CL_DEV, ends, 0)
    chain[n_rows] = jnp.zeros((B, HALF), F32)
    loads[2].wait()

    def take_left(a, carry):
        high, low = split(left_raw[a].T)
        left[a, :B, :] = high
        left[a, B:, :] = low
        return carry

    lax.fori_loop(0, n_rows, take_left, 0)
    gather_forward(0)
    loads[3].wait()

    def take_near(o, carry):
        for s in range(NEAR_DEV):
            high, low = split(near_raw[o, s])
            near[o, :B, s * B : (s + 1) * B] = high
            near[o, B:, s * B : (s + 1) * B] = low
        return carry

    lax.fori_loop(0, CL_DEV, take_near, 0)

    def take_halo(q, halo):
        def step(j, carry):
            put(q, lax.rem(j + 24, 32), halo[q, lax.div(j, 2), lax.rem(j, 2)])
            return carry

        lax.fori_loop(0, CL_DEV, step, 0)

    gather_end(0)
    take_halo(0, halo_b)
    base = me * CL_DEV - 8

    def near_term(q):
        def step(g, carry):
            for o in [g * 4 + j for j in range(4)]:
                picked = [vcat[q, jnp.clip(cols_ref[s, o] - base, 0, 31)] for s in range(NEAR_DEV)]
                acc[q, o] = quadrants(jnp.dot(near[o], jnp.concatenate(picked, axis=0), preferred_element_type=F32))
            return carry

        lax.fori_loop(0, CL_DEV // 4, step, 0)

    def far_term(ap, q, first, end):
        def step(g, carry):
            several(g)
            return carry

        def several(g, skip=0):
            ks = [g * UNROLL + j for j in range(UNROLL)]
            for k in ks[skip:]:
                a2a(ap, q, k).wait_recv()
            here = []
            for k in ks:
                both = jnp.concatenate(split(coef_in[ap, q, k]), axis=1)
                here.append(quadrants(jnp.dot(left[behind(k)], both, preferred_element_type=F32)))
            for k, item in zip(ks, here):
                chain[k] = item + chain[prev[k]]

        if first == 0:
            several(0, 1)
        lax.fori_loop(max(first // UNROLL, 1), end // UNROLL, step, 0)

    near_term(0)
    far_term(0, 0, 0, n_rows)

    def finish_rows(q):
        def step(o, carry):
            part[q, lax.div(o, 4), lax.rem(lax.div(o, 2), 2), lax.rem(o, 2)] = acc[q, o] + chain[last[o]]
            return carry

        lax.fori_loop(0, CL_DEV, step, 0)

    def rows_sib(q, d):
        to_y = lax.rem(my_y + d, FAR_Y)
        return remote(part.at[q, to_y, 1 - my_c], sib_in.at[q, d], rss_s.at[q, d], rss_r.at[q, d], me, sib)

    def rows_y(q, d):
        return remote(mix.at[q, d], y_in.at[q, d], rsy_s.at[q, d], rsy_r.at[q, d], me, y_peer(d))

    def rows_start(q):
        for d in (2, 1, 3, 0):
            rows_sib(q, d).start()

    def rows_send(q):
        for d in (2, 1, 3):
            rows_sib(q, d).wait_recv()
            mix[q, d] = part[q, lax.rem(my_y + d, FAR_Y), my_c] + sib_in[q, d]
            rows_y(q, d).start()
        rows_sib(q, 0).wait_recv()

    def rows_own(q):
        for d in (1, 2, 3):
            rows_y(q, d).wait_recv()
        own_u[q, far] = (part[q, my_y, my_c] + sib_in[q, 0]) + (y_in[q, 1] + y_in[q, 2] + y_in[q, 3])

    def take_own(q):
        def step(j, carry):
            put(q, j + 8, own_u[q, lax.div(j, 2), lax.rem(j, 2)])
            return carry

        lax.fori_loop(0, CL_DEV, step, 0)

    finish_rows(0)
    rows_start(0)
    rows_send(0)
    gather_forward(5)
    gather_end(5)
    take_halo(1, halo_b)
    near_term(1)
    rows_own(0)
    halo_copy(1).start()
    gather_start(1)
    gather_forward(1)
    gather_end(1)
    take_own(0)
    send_coefficients(1, 0)

    far_term(0, 1, 0, n_rows)
    finish_rows(1)
    rows_start(1)
    rows_send(1)
    halo_copy(1).wait_recv()
    rows_own(1)
    halo_copy(2).start()
    gather_start(2)
    gather_start(3)
    gather_forward(2)
    gather_end(2)
    take_own(1)
    send_coefficients(1, 1)
    gather_forward(3)
    halo_copy(2).wait_recv()
    gather_start(4)
    gather_end(3)
    take_halo(0, halo_u)
    near_term(0)

    def finish_columns(q, h):
        def step(g, carry):
            for o in [h * 8 + g * 4 + j for j in range(4)]:
                tile = (acc[q, o] + chain[last[o]]).T
                lanes = pl.ds(pl.multiple_of((g * 4 + o % 4) * B, B), B)
                for j in range(4):
                    part_t[q, h, j // 2, j % 2, :, lanes] = tile[32 * j : 32 * j + 32]
            return carry

        for g in range(2):
            step(g, 0)

    def columns_sib(q, h):
        return remote(part_t.at[q, h, :, 1 - my_c], sib_t.at[q, h], rts_s.at[q, h], rts_r.at[q, h], me, sib)

    def columns_y(q, h, j):
        to_y = q + 2 * j
        d = lax.rem(to_y + FAR_Y - my_y, FAR_Y)
        return remote(mix_t.at[q, h, j], y_t.at[h, d], rty_s.at[q, h, j], rty_r.at[h, d], me, to_y * 2 + my_c)

    def columns_send(q, h):
        for j in range(2):
            @pl.when(my_y != q + 2 * j)
            def _():
                mix_t[q, h, j] = part_t[q, h, j, my_c] + sib_t[q, h, j]
                columns_y(q, h, j).start()

    def columns_own(q, h):
        for j in range(2):
            @pl.when(my_y == q + 2 * j)
            def _():
                for d in (1, 2, 3):
                    remote(mix_t.at[q, h, j], y_t.at[h, d], rty_s.at[q, h, j], rty_r.at[h, d], me, y_peer(d)).wait_recv()
                mine = (part_t[q, h, j, my_c] + sib_t[q, h, j]) + (y_t[h, 1] + y_t[h, 2] + y_t[h, 3])
                own_w[:, h * ROW_HALF : (h + 1) * ROW_HALF] = mine

    far_term(1, 0, 0, n_rows)
    for h in range(2):
        finish_columns(0, h)
        columns_sib(0, h).start()
    gather_forward(4)
    for h in range(2):
        columns_sib(0, h).wait_recv()
        columns_send(0, h)
    gather_end(4)
    take_halo(1, halo_u)
    near_term(1)
    my_half = lax.rem(my_y, 2)

    def turn(o, carry):
        lanes = pl.ds(pl.multiple_of(o * B, B), B)
        turned[0, :, lanes] = side[o, :, pl.ds(pl.multiple_of(my_half * HALF, HALF), HALF)].T
        turned[1, :, lanes] = own_u[my_half, lax.div(o, 2), lax.rem(o, 2)].T
        return carry

    lax.fori_loop(0, CL_DEV, turn, 0)
    for h in range(2):
        columns_own(0, h)
    mine = pl.ds(pl.multiple_of((lax.div(my_y, 2) * 2 + my_c) * 32, 32), 32)
    lane = lax.broadcasted_iota(jnp.int32, (32, B), 1)

    def dots(pairs):
        def step(o, sums):
            lanes = pl.ds(pl.multiple_of(o * B, B), B)
            items = (turned[0, mine, lanes], turned[1, mine, lanes], own_w[:, lanes] if pairs[-1][1] == 2 else None)
            return tuple(total + items[i] * items[j] for total, (i, j) in zip(sums, pairs))

        sums = lax.fori_loop(0, CL_DEV, step, tuple(jnp.zeros((32, B), F32) for _ in pairs))
        return [jnp.sum(item, axis=1, keepdims=True) for item in sums]

    early = dots(((0, 0), (0, 1), (1, 1)))
    for q in range(2):
        lax.fori_loop(1, n_rows, lambda k, carry: settle(0, q, k), 0)
    far_term(1, 1, 0, n_rows)
    for h in range(2):
        finish_columns(1, h)
        columns_sib(1, h).start()
    for h in range(2):
        columns_sib(1, h).wait_recv()
        columns_send(1, h)
    for q in range(2):
        lax.fori_loop(1, n_rows, lambda k, carry: settle(1, q, k), 0)
    for g in (1, 2, 3, 4):
        halo_copy(g).wait_send()
    for g in range(6):
        for d in range(FAR_Y):
            if d > 0:
                gather_y(g, d).wait_send()
            gather_sib(g, d).wait_send()
    for q in range(2):
        for d in range(FAR_Y):
            rows_sib(q, d).wait_send()
        for d in (1, 2, 3):
            rows_y(q, d).wait_send()
        for h in range(2):
            columns_sib(q, h).wait_send()
    for h in range(2):
        for j in range(2):
            @pl.when(my_y != 2 * j)
            def _():
                columns_y(0, h, j).wait_send()
    for h in range(2):
        columns_own(1, h)

    table = jnp.zeros((32, B), F32)
    for j, item in enumerate(early + dots(((0, 2), (1, 2), (2, 2)))):
        table = jnp.where(lane == j, item, table)
    flat = jnp.concatenate([table, jnp.zeros((B - 32, B), F32)], axis=0).T[:8]
    gram_out[0] = flat

    def gram(k):
        return remote(gram_out.at[0 if k < ROW_X else 1], gram_in.at[k], gram_s.at[k], gram_r.at[k], ahead(k), far)

    along_x = list(range(1, ROW_X))
    along_z = [ROW_X * dz for dz in range(1, n_z)]
    total = flat
    for k in along_x:
        gram(k).start()
    for k in along_x:
        gram(k).wait_recv()
    for k in along_x:
        total = total + gram_in[k]
    gram_out[1] = total
    for k in along_z:
        gram(k).start()
    for k in along_z:
        gram(k).wait_recv()
    for k in along_z:
        total = total + gram_in[k]
    weights = combine([total[j : j + 1] for j in range(6)])
    stack = jnp.concatenate(list(weights) + [jnp.zeros((B - 5, B), F32)], axis=0).T
    parts = [stack[:32, j : j + 1] for j in range(5)]
    b, u, w = turned[0, mine, :], turned[1, mine, :], own_w[...]
    sol_ref[...] = parts[0] * b + parts[1] * u
    res_ref[...] = parts[2] * b + parts[3] * u + parts[4] * w

    for k in along_x + along_z:
        gram(k).wait_send()
    for h in range(2):
        for j in range(2):
            @pl.when(my_y != 1 + 2 * j)
            def _():
                columns_y(1, h, j).wait_send()


def deliver(sol_in, res_in, sol_out, res_out):
    sol_out[...] = sol_in[...]
    res_out[...] = res_in[...]


def solution(mesh):
    n_rows = mesh.shape["rows"]
    dma = pltpu.SemaphoreType.DMA

    def shards(right_side, near_blocks, near_cols, far_src, far_tgt, far_left, far_right):
        anywhere = pl.BlockSpec(memory_space=pl.ANY)
        scalars = pl.BlockSpec(memory_space=pltpu.SMEM)
        vector = pl.BlockSpec(memory_space=pltpu.VMEM)
        sol, res = pl.pallas_call(
            functools.partial(kernel, n_rows),
            out_shape=(jax.ShapeDtypeStruct((32, CL_DEV * B), F32),) * 2,
            in_specs=[scalars] * 3 + [anywhere] * 4,
            out_specs=(vector, vector),
            scratch_shapes=[
                pltpu.VMEM((CL_DEV, B, 2 * HALF), F32),
                pltpu.VMEM((CL_DEV, NEAR_DEV, B, B), F32),
                pltpu.VMEM((CL_DEV, 2 * B, NEAR_DEV * B), BF16),
                pltpu.VMEM((n_rows, R, B), F32),
                pltpu.VMEM((n_rows, 2 * B, R), BF16),
                pltpu.VMEM((n_rows, R, B), F32),
                pltpu.VMEM((n_rows, 2 * R, B), BF16),
                pltpu.VMEM((2, 32, B, 2 * HALF), BF16),
                pltpu.VMEM((2, 2, n_rows, R, HALF), F32),
                pltpu.VMEM((2, 2, n_rows, R, HALF), F32),
                pltpu.VMEM((2, 8, 2, B, HALF), F32),
                pltpu.VMEM((2, 8, 2, B, HALF), F32),
                pltpu.VMEM((2, 8, 2, B, HALF), F32),
                pltpu.VMEM((2, CL_DEV, B, HALF), F32),
                pltpu.VMEM((n_rows + 1, B, HALF), F32),
                pltpu.VMEM((2, 4, 2, 2, B, HALF), F32),
                pltpu.VMEM((2, 2, 2, 2, 32, ROW_HALF), F32),
                pltpu.VMEM((2, 4, 2, B, HALF), F32),
                pltpu.VMEM((2, 4, 2, B, HALF), F32),
                pltpu.VMEM((2, 4, 2, B, HALF), F32),
                pltpu.VMEM((2, 2, 2, 32, ROW_HALF), F32),
                pltpu.VMEM((2, 2, 2, 32, ROW_HALF), F32),
                pltpu.VMEM((2, 4, 32, ROW_HALF), F32),
                pltpu.VMEM((2, HALF, CL_DEV * B), F32),
                pltpu.VMEM((32, CL_DEV * B), F32),
                pltpu.VMEM((2, 8, B), F32),
                pltpu.VMEM((n_rows, 8, B), F32),
                pltpu.SMEM((n_rows,), jnp.int32),
                pltpu.SMEM((CL_DEV,), jnp.int32),
                dma((4,)), dma((2, 2, n_rows)), dma((2, 2, n_rows)), dma((5,)), dma((5,)),
                dma((6, 4)), dma((6, 4)), dma((6, 4)), dma((6, 4)),
                dma((2, 4)), dma((2, 4)), dma((2, 4)), dma((2, 4)),
                dma((2, 2)), dma((2, 2)), dma((2, 2, 2)), dma((2, 4)),
                dma((n_rows,)), dma((n_rows,)),
            ],
            compiler_params=pltpu.CompilerParams(collective_id=0, has_side_effects=True, vmem_limit_bytes=60 << 20),
            name="gmres",
        )(
            near_cols.T,
            far_src.reshape(n_rows),
            far_tgt.reshape(n_rows),
            right_side.reshape(CL_DEV, B, 2 * HALF),
            near_blocks,
            jnp.swapaxes(far_left.reshape(n_rows, B, R), 1, 2),
            jnp.swapaxes(far_right.reshape(n_rows, B, R), 1, 2),
        )
        sol, res = pl.pallas_call(
            deliver,
            out_shape=(jax.ShapeDtypeStruct((32, CL_DEV * B), F32),) * 2,
            in_specs=[vector] * 2,
            out_specs=(vector, vector),
            name="deliver",
        )(sol, res)
        return sol.T, res.T

    return jax.shard_map(
        shards,
        mesh=mesh,
        in_specs=(
            P("rows", None),
            P("rows", "far", None, None),
            P("rows", "far"),
            P("rows", None, "far"),
            P("rows", None, "far"),
            P("rows", None, "far", None, None),
            P("rows", None, "far", None, None),
        ),
        out_specs=(P("rows", "far"), P("rows", "far")),
        check_vma=False,
    )
```

```python
import functools

import jax
import jax.numpy as jnp
from jax import lax
from jax.experimental import pallas as pl
from jax.experimental.pallas import tpu as pltpu
from jax.sharding import PartitionSpec as P

B = 128
R = 64
HALF = 128
NEAR_DEV = 6
CL_DEV = 16
ROW_X = 4
FAR_Y = 4
UNROLL = 8
ROW_HALF = 1024
EPS = 1e-06
MESH = pl.DeviceIdType.MESH
F32 = jnp.float32
BF16 = jnp.bfloat16


def split(value):
    high = value.astype(BF16)
    return high, (value - high.astype(F32)).astype(BF16)


def quadrants(value):
    rows = value.shape[0] // 2
    return (value[:rows, :HALF] + value[:rows, HALF:]) + (value[rows:, :HALF] + value[rows:, HALF:])


def interleave(value):
    lane = lax.broadcasted_iota(jnp.int32, (value.shape[0], HALF), 1)
    first, second = value[:, :HALF], value[:, HALF:]
    return jnp.where(lane < 64, first, pltpu.roll(second, 64, 1)), jnp.where(lane < 64, pltpu.roll(first, 64, 1), second)


def combine(gram):
    bb, bu, uu, bw, uw, ww = gram
    length_sq = bb + EPS
    length = jnp.sqrt(length_sq)
    unit = bb / length_sq
    gap = EPS / length_sq
    p1, q11, p2, q12, q22 = bu / length_sq, uu / length_sq, bw / length_sq, uw / length_sq, ww / length_sq
    upper_left = 0.5 * unit + p1
    alpha = p1 - 0.5 * gap
    cand_sq = jnp.maximum(q11 - 2.0 * alpha * p1 + alpha * alpha * unit, 0.0)
    lower_sq = cand_sq + EPS
    lower_left = jnp.sqrt(lower_sq)
    f_s = (p1 - alpha * unit) / lower_left
    f_ns = (p2 - alpha * p1) / lower_left
    s_s = cand_sq / lower_sq
    s_ns = (q12 - alpha * q11 - alpha * p2 + alpha * alpha * p1) / lower_sq
    ns_ns = (q22 - 2.0 * alpha * q12 + alpha * alpha * q11) / lower_sq
    top = 0.5 * f_s + f_ns
    mid = 0.5 * s_s + s_ns
    beta = s_ns - 0.5 * EPS / lower_sq
    rest_sq = ns_ns + top * top * unit + beta * beta * s_s - 2.0 * top * f_ns - 2.0 * beta * s_ns + 2.0 * top * beta * f_s
    lower_right = jnp.sqrt(jnp.maximum(rest_sq, 0.0) + EPS)
    radius_one = jnp.sqrt(upper_left * upper_left + lower_left * lower_left)
    cosine_one = upper_left / radius_one
    sine_one = lower_left / radius_one
    rotated_top = cosine_one * length
    rotated_mid = -sine_one * length
    coupled = cosine_one * top + sine_one * mid
    diagonal_two = cosine_one * mid - sine_one * top
    radius_two = jnp.sqrt(diagonal_two * diagonal_two + lower_right * lower_right)
    weight_two = diagonal_two * rotated_mid / (radius_two * radius_two)
    weight_one = (rotated_top - coupled * weight_two) / radius_one
    one = weight_one / length
    two = weight_two / (lower_left * length)
    sol_b = one - alpha * two
    return sol_b, two, 1.0 - 0.5 * sol_b, -0.5 * two - one + alpha * two, -two


def kernel(
    n_rows,
    cols_ref, src_ref, tgt_ref, side_hbm, near_hbm, left_hbm, right_hbm,
    sol_ref, res_ref,
    side, near_raw, near, left_raw, left, right_raw, right, vcat, coef_out, coef_in,
    halo_b, own_u, halo_u, acc, chain, part, part_t,
    sib_in, mix, y_in, sib_t, mix_t, y_t, turned, own_w, gram_out, gram_in,
    prev, last,
    load_sem, a2a_s, a2a_r, halo_s, halo_r, agy_s, agy_r, ags_s, ags_r,
    rss_s, rss_r, rsy_s, rsy_r, rts_s, rts_r, rty_s, rty_r, gram_s, gram_r,
):
    n_z = n_rows // ROW_X
    me = lax.axis_index("rows")
    far = lax.axis_index("far")
    my_x, my_z = lax.rem(me, ROW_X), lax.div(me, ROW_X)
    my_y, my_c = lax.div(far, 2), lax.rem(far, 2)
    sib = my_y * 2 + 1 - my_c

    def ahead(k):
        return lax.rem(my_z + lax.div(k, ROW_X), n_z) * ROW_X + lax.rem(my_x + lax.rem(k, ROW_X), ROW_X)

    def behind(k):
        return lax.rem(my_z + n_z - lax.div(k, ROW_X), n_z) * ROW_X + lax.rem(my_x + ROW_X - lax.rem(k, ROW_X), ROW_X)

    def y_peer(d):
        return lax.rem(my_y + d, FAR_Y) * 2 + my_c

    def y_from(d):
        return lax.rem(my_y + FAR_Y - d, FAR_Y) * 2 + my_c

    def remote(src, dst, send, recv, rows, to_far):
        return pltpu.make_async_remote_copy(
            src_ref=src, dst_ref=dst, send_sem=send, recv_sem=recv,
            device_id={"rows": rows, "far": to_far}, device_id_type=MESH,
        )

    loads = [
        pltpu.make_async_copy(side_hbm, side, load_sem.at[0]),
        pltpu.make_async_copy(right_hbm, right_raw, load_sem.at[1]),
        pltpu.make_async_copy(left_hbm, left_raw, load_sem.at[2]),
        pltpu.make_async_copy(near_hbm, near_raw, load_sem.at[3]),
    ]
    for load in loads:
        load.start()

    barrier = pltpu.get_barrier_semaphore()

    def greet(k, carry):
        pl.semaphore_signal(barrier, inc=1, device_id={"rows": ahead(k), "far": far}, device_id_type=MESH)
        return carry

    lax.fori_loop(1, n_rows, greet, 0)
    for d in (1, 2, 3):
        pl.semaphore_signal(barrier, inc=1, device_id={"rows": me, "far": y_peer(d)}, device_id_type=MESH)
    pl.semaphore_signal(barrier, inc=1, device_id={"rows": me, "far": sib}, device_id_type=MESH)

    loads[0].wait()

    def put(q, slot, value):
        high, low = split(value)
        vcat[q, slot, :, :HALF] = high
        vcat[q, slot, :, HALF:] = low

    def take_side(o, carry):
        for q, item in enumerate(interleave(side[o])):
            put(q, o + 8, item)
            side[o, :, q * HALF : (q + 1) * HALF] = item
        return carry

    lax.fori_loop(0, CL_DEV, take_side, 0)
    loads[1].wait()

    def take_right(t, carry):
        high, low = split(right_raw[t])
        right[t, :R, :] = high
        right[t, R:, :] = low
        return carry

    lax.fori_loop(0, n_rows, take_right, 0)
    pl.semaphore_wait(barrier, n_rows + 3)

    halo_to = (lax.rem(me + n_rows - 1, n_rows), lax.rem(me + 1, n_rows))

    def halo_copy(g, i):
        if g >= 3:
            rows = side.at[far + 8 * i, :, pl.ds((g - 3) * HALF, HALF)]
            return remote(rows, halo_b.at[g - 3, far, i], halo_s.at[g, i], halo_r.at[g, i], halo_to[i], far)
        return remote(own_u.at[g - 1, far, i], halo_u.at[g - 1, far, i], halo_s.at[g, i], halo_r.at[g, i], halo_to[i], far)

    def halo_start(g):
        for i in range(2):
            halo_copy(g, i).start()

    def halo_wait(g):
        for i in range(2):
            halo_copy(g, i).wait_recv()

    halo_start(3)
    halo_start(4)

    def a2a(ap, q, k):
        return remote(coef_out.at[ap, q, k], coef_in.at[ap, q, k], a2a_s.at[ap, q, k], a2a_r.at[ap, q, k], ahead(k), far)

    def settle(ap, q, k):
        a2a(ap, q, k).wait_send()
        return 0

    def coefficient(q, t):
        return quadrants(jnp.dot(right[t], vcat[q, src_ref[t] + 8], preferred_element_type=F32))

    def send_coefficients(ap, q):
        def step(g, carry):
            for k in [g * UNROLL + j for j in range(UNROLL)]:
                coef_out[ap, q, k] = coefficient(q, ahead(k))
                a2a(ap, q, k).start()
            return carry

        lax.fori_loop(1, n_rows // UNROLL, step, 0)
        coef_in[ap, q, 0] = coefficient(q, me)
        for k in range(1, UNROLL):
            coef_out[ap, q, k] = coefficient(q, ahead(k))
            a2a(ap, q, k).start()

    send_coefficients(0, 0)
    send_coefficients(0, 1)

    def group_ref(g, who):
        if g in (0, 5):
            return halo_b.at[g // 5, who]
        if g <= 2:
            return own_u.at[g - 1, who]
        return halo_u.at[g - 3, who]

    def gather_y(g, d):
        ref = group_ref(g, far)
        return remote(ref, ref, agy_s.at[g, d], agy_r.at[g, d], me, y_peer(d))

    def gather_sib(g, d):
        ref = group_ref(g, y_from(d))
        return remote(ref, ref, ags_s.at[g, d], ags_r.at[g, d], me, sib)

    def gather_start(g):
        for d in (2, 1, 3):
            gather_y(g, d).start()
        gather_sib(g, 0).start()

    def gather_forward(g):
        for d in (1, 3, 2):
            ref = group_ref(g, y_from(d))
            remote(ref, ref, agy_s.at[g, d], agy_r.at[g, d], me, y_peer(d)).wait_recv()
            gather_sib(g, d).start()

    def gather_end(g):
        for d in range(FAR_Y):
            ref = group_ref(g, lax.rem(my_y + FAR_Y - d, FAR_Y) * 2 + 1 - my_c)
            remote(ref, ref, ags_s.at[g, d], ags_r.at[g, d], me, sib).wait_recv()

    for q in range(2):
        halo_wait(q + 3)
        gather_start(q * 5)

    def tables(k, carry):
        mine = tgt_ref[behind(k)]
        found = n_rows
        for j in range(n_rows):
            same = jnp.logical_and(tgt_ref[behind(j)] == mine, j < k)
            found = jnp.where(same, j, found)
        prev[k] = found
        return carry

    lax.fori_loop(0, n_rows, tables, 0)

    def ends(o, carry):
        found = n_rows
        for j in range(n_rows):
            found = jnp.where(tgt_ref[behind(j)] == o, j, found)
        last[o] = found
        return carry

    lax.fori_loop(0, CL_DEV, ends, 0)
    chain[n_rows] = jnp.zeros((B, HALF), F32)
    loads[2].wait()

    def take_left(a, carry):
        high, low = split(left_raw[a].T)
        left[a, :B, :] = high
        left[a, B:, :] = low
        return carry

    lax.fori_loop(0, n_rows, take_left, 0)
    gather_forward(0)
    loads[3].wait()

    def take_near(o, carry):
        for s in range(NEAR_DEV):
            high, low = split(near_raw[o, s])
            near[o, :B, s * B : (s + 1) * B] = high
            near[o, B:, s * B : (s + 1) * B] = low
        return carry

    lax.fori_loop(0, CL_DEV, take_near, 0)

    def take_halo(q, halo):
        def step(j, carry):
            who, i = lax.rem(j, 8), lax.div(j, 8)
            put(q, who + 24 * (1 - i), halo[q, who, i])
            return carry

        lax.fori_loop(0, CL_DEV, step, 0)

    gather_end(0)
    take_halo(0, halo_b)
    base = me * CL_DEV - 8

    def near_term(q):
        def step(g, carry):
            for o in [g * 4 + j for j in range(4)]:
                picked = [vcat[q, jnp.clip(cols_ref[s, o] - base, 0, 31)] for s in range(NEAR_DEV)]
                acc[q, o] = quadrants(jnp.dot(near[o], jnp.concatenate(picked, axis=0), preferred_element_type=F32))
            return carry

        lax.fori_loop(0, CL_DEV // 4, step, 0)

    def far_term(ap, q, first, end):
        def step(g, carry):
            several(g)
            return carry

        def several(g, skip=0):
            ks = [g * UNROLL + j for j in range(UNROLL)]
            for k in ks[skip:]:
                a2a(ap, q, k).wait_recv()
            here = []
            for k in ks:
                both = jnp.concatenate(split(coef_in[ap, q, k]), axis=1)
                here.append(quadrants(jnp.dot(left[behind(k)], both, preferred_element_type=F32)))
            for k, item in zip(ks, here):
                chain[k] = item + chain[prev[k]]

        if first == 0:
            several(0, 1)
        lax.fori_loop(max(first // UNROLL, 1), end // UNROLL, step, 0)

    near_term(0)
    far_term(0, 0, 0, n_rows)

    def finish_rows(q):
        def step(o, carry):
            part[q, lax.div(o, 8), lax.rem(lax.div(o, 2), 4), lax.rem(o, 2)] = acc[q, o] + chain[last[o]]
            return carry

        lax.fori_loop(0, CL_DEV, step, 0)

    def rows_sib(q, d):
        to_y = lax.rem(my_y + d, FAR_Y)
        return remote(part.at[q, :, to_y, 1 - my_c], sib_in.at[q, d], rss_s.at[q, d], rss_r.at[q, d], me, sib)

    def rows_y(q, d):
        return remote(mix.at[q, d], y_in.at[q, d], rsy_s.at[q, d], rsy_r.at[q, d], me, y_peer(d))

    def rows_start(q):
        for d in (2, 1, 3, 0):
            rows_sib(q, d).start()

    def rows_send(q):
        for d in (2, 1, 3):
            rows_sib(q, d).wait_recv()
            mix[q, d] = part[q, :, lax.rem(my_y + d, FAR_Y), my_c] + sib_in[q, d]
            rows_y(q, d).start()
        rows_sib(q, 0).wait_recv()

    def rows_own(q):
        for d in (1, 2, 3):
            rows_y(q, d).wait_recv()
        own_u[q, far] = (part[q, :, my_y, my_c] + sib_in[q, 0]) + (y_in[q, 1] + y_in[q, 2] + y_in[q, 3])

    def take_own(q):
        def step(j, carry):
            put(q, j + 8, own_u[q, lax.rem(j, 8), lax.div(j, 8)])
            return carry

        lax.fori_loop(0, CL_DEV, step, 0)

    finish_rows(0)
    rows_start(0)
    rows_send(0)
    gather_forward(5)
    gather_end(5)
    take_halo(1, halo_b)
    near_term(1)
    rows_own(0)
    halo_start(1)
    gather_start(1)
    gather_forward(1)
    gather_end(1)
    take_own(0)
    send_coefficients(1, 0)

    far_term(0, 1, 0, n_rows)
    finish_rows(1)
    rows_start(1)
    rows_send(1)
    halo_wait(1)
    rows_own(1)
    halo_start(2)
    gather_start(2)
    gather_start(3)
    gather_forward(2)
    gather_end(2)
    take_own(1)
    send_coefficients(1, 1)
    gather_forward(3)
    halo_wait(2)
    gather_start(4)
    gather_end(3)
    take_halo(0, halo_u)
    near_term(0)

    def finish_columns(q, h):
        def step(g, carry):
            for o in [h * 8 + g * 4 + j for j in range(4)]:
                tile = (acc[q, o] + chain[last[o]]).T
                lanes = pl.ds(pl.multiple_of((g * 4 + o % 4) * B, B), B)
                for j in range(4):
                    part_t[q, h, j // 2, j % 2, :, lanes] = tile[32 * j : 32 * j + 32]
            return carry

        for g in range(2):
            step(g, 0)

    def columns_sib(q, h):
        return remote(part_t.at[q, h, :, 1 - my_c], sib_t.at[q, h], rts_s.at[q, h], rts_r.at[q, h], me, sib)

    def columns_y(q, h, j):
        to_y = q + 2 * j
        d = lax.rem(to_y + FAR_Y - my_y, FAR_Y)
        return remote(mix_t.at[q, h, j], y_t.at[h, d], rty_s.at[q, h, j], rty_r.at[h, d], me, to_y * 2 + my_c)

    def columns_send(q, h):
        for j in range(2):
            @pl.when(my_y != q + 2 * j)
            def _():
                mix_t[q, h, j] = part_t[q, h, j, my_c] + sib_t[q, h, j]
                columns_y(q, h, j).start()

    def columns_own(q, h):
        for j in range(2):
            @pl.when(my_y == q + 2 * j)
            def _():
                for d in (1, 2, 3):
                    remote(mix_t.at[q, h, j], y_t.at[h, d], rty_s.at[q, h, j], rty_r.at[h, d], me, y_peer(d)).wait_recv()
                mine = (part_t[q, h, j, my_c] + sib_t[q, h, j]) + (y_t[h, 1] + y_t[h, 2] + y_t[h, 3])
                own_w[:, h * ROW_HALF : (h + 1) * ROW_HALF] = mine

    far_term(1, 0, 0, n_rows)
    for h in range(2):
        finish_columns(0, h)
        columns_sib(0, h).start()
    gather_forward(4)
    for h in range(2):
        columns_sib(0, h).wait_recv()
        columns_send(0, h)
    gather_end(4)
    take_halo(1, halo_u)
    near_term(1)
    my_half = lax.rem(my_y, 2)

    def turn(o, carry):
        lanes = pl.ds(pl.multiple_of(o * B, B), B)
        turned[0, :, lanes] = side[o, :, pl.ds(pl.multiple_of(my_half * HALF, HALF), HALF)].T
        turned[1, :, lanes] = own_u[my_half, lax.rem(o, 8), lax.div(o, 8)].T
        return carry

    lax.fori_loop(0, CL_DEV, turn, 0)
    for h in range(2):
        columns_own(0, h)
    mine = pl.ds(pl.multiple_of((lax.div(my_y, 2) * 2 + my_c) * 32, 32), 32)
    lane = lax.broadcasted_iota(jnp.int32, (32, B), 1)

    def dots(pairs):
        def step(o, sums):
            lanes = pl.ds(pl.multiple_of(o * B, B), B)
            items = (turned[0, mine, lanes], turned[1, mine, lanes], own_w[:, lanes] if pairs[-1][1] == 2 else None)
            return tuple(total + items[i] * items[j] for total, (i, j) in zip(sums, pairs))

        sums = lax.fori_loop(0, CL_DEV, step, tuple(jnp.zeros((32, B), F32) for _ in pairs))
        return [jnp.sum(item, axis=1, keepdims=True) for item in sums]

    early = dots(((0, 0), (0, 1), (1, 1)))
    for q in range(2):
        lax.fori_loop(1, n_rows, lambda k, carry: settle(0, q, k), 0)
    far_term(1, 1, 0, n_rows)
    for h in range(2):
        finish_columns(1, h)
        columns_sib(1, h).start()
    for h in range(2):
        columns_sib(1, h).wait_recv()
        columns_send(1, h)
    for q in range(2):
        lax.fori_loop(1, n_rows, lambda k, carry: settle(1, q, k), 0)
    for g in (1, 2, 3, 4):
        for i in range(2):
            halo_copy(g, i).wait_send()
    for g in range(6):
        for d in range(FAR_Y):
            if d > 0:
                gather_y(g, d).wait_send()
            gather_sib(g, d).wait_send()
    for q in range(2):
        for d in range(FAR_Y):
            rows_sib(q, d).wait_send()
        for d in (1, 2, 3):
            rows_y(q, d).wait_send()
        for h in range(2):
            columns_sib(q, h).wait_send()
    for h in range(2):
        for j in range(2):
            @pl.when(my_y != 2 * j)
            def _():
                columns_y(0, h, j).wait_send()
    for h in range(2):
        columns_own(1, h)

    table = jnp.zeros((32, B), F32)
    for j, item in enumerate(early + dots(((0, 2), (1, 2), (2, 2)))):
        table = jnp.where(lane == j, item, table)
    flat = jnp.concatenate([table, jnp.zeros((B - 32, B), F32)], axis=0).T[:8]
    gram_out[0] = flat

    def gram(k):
        return remote(gram_out.at[0 if k < ROW_X else 1], gram_in.at[k], gram_s.at[k], gram_r.at[k], ahead(k), far)

    along_x = list(range(1, ROW_X))
    along_z = [ROW_X * dz for dz in range(1, n_z)]
    total = flat
    for k in along_x:
        gram(k).start()
    for k in along_x:
        gram(k).wait_recv()
    for k in along_x:
        total = total + gram_in[k]
    gram_out[1] = total
    for k in along_z:
        gram(k).start()
    for k in along_z:
        gram(k).wait_recv()
    for k in along_z:
        total = total + gram_in[k]
    weights = combine([total[j : j + 1] for j in range(6)])
    stack = jnp.concatenate(list(weights) + [jnp.zeros((B - 5, B), F32)], axis=0).T
    parts = [stack[:32, j : j + 1] for j in range(5)]
    b, u, w = turned[0, mine, :], turned[1, mine, :], own_w[...]
    sol_ref[...] = parts[0] * b + parts[1] * u
    res_ref[...] = parts[2] * b + parts[3] * u + parts[4] * w

    for k in along_x + along_z:
        gram(k).wait_send()
    for h in range(2):
        for j in range(2):
            @pl.when(my_y != 1 + 2 * j)
            def _():
                columns_y(1, h, j).wait_send()


def deliver(sol_in, res_in, sol_out, res_out):
    sol_out[...] = sol_in[...]
    res_out[...] = res_in[...]


def solution(mesh):
    n_rows = mesh.shape["rows"]
    dma = pltpu.SemaphoreType.DMA

    def shards(right_side, near_blocks, near_cols, far_src, far_tgt, far_left, far_right):
        anywhere = pl.BlockSpec(memory_space=pl.ANY)
        scalars = pl.BlockSpec(memory_space=pltpu.SMEM)
        vector = pl.BlockSpec(memory_space=pltpu.VMEM)
        sol, res = pl.pallas_call(
            functools.partial(kernel, n_rows),
            out_shape=(jax.ShapeDtypeStruct((32, CL_DEV * B), F32),) * 2,
            in_specs=[scalars] * 3 + [anywhere] * 4,
            out_specs=(vector, vector),
            scratch_shapes=[
                pltpu.VMEM((CL_DEV, B, 2 * HALF), F32),
                pltpu.VMEM((CL_DEV, NEAR_DEV, B, B), F32),
                pltpu.VMEM((CL_DEV, 2 * B, NEAR_DEV * B), BF16),
                pltpu.VMEM((n_rows, R, B), F32),
                pltpu.VMEM((n_rows, 2 * B, R), BF16),
                pltpu.VMEM((n_rows, R, B), F32),
                pltpu.VMEM((n_rows, 2 * R, B), BF16),
                pltpu.VMEM((2, 32, B, 2 * HALF), BF16),
                pltpu.VMEM((2, 2, n_rows, R, HALF), F32),
                pltpu.VMEM((2, 2, n_rows, R, HALF), F32),
                pltpu.VMEM((2, 8, 2, B, HALF), F32),
                pltpu.VMEM((2, 8, 2, B, HALF), F32),
                pltpu.VMEM((2, 8, 2, B, HALF), F32),
                pltpu.VMEM((2, CL_DEV, B, HALF), F32),
                pltpu.VMEM((n_rows + 1, B, HALF), F32),
                pltpu.VMEM((2, 2, 4, 2, B, HALF), F32),
                pltpu.VMEM((2, 2, 2, 2, 32, ROW_HALF), F32),
                pltpu.VMEM((2, 4, 2, B, HALF), F32),
                pltpu.VMEM((2, 4, 2, B, HALF), F32),
                pltpu.VMEM((2, 4, 2, B, HALF), F32),
                pltpu.VMEM((2, 2, 2, 32, ROW_HALF), F32),
                pltpu.VMEM((2, 2, 2, 32, ROW_HALF), F32),
                pltpu.VMEM((2, 4, 32, ROW_HALF), F32),
                pltpu.VMEM((2, HALF, CL_DEV * B), F32),
                pltpu.VMEM((32, CL_DEV * B), F32),
                pltpu.VMEM((2, 8, B), F32),
                pltpu.VMEM((n_rows, 8, B), F32),
                pltpu.SMEM((n_rows,), jnp.int32),
                pltpu.SMEM((CL_DEV,), jnp.int32),
                dma((4,)), dma((2, 2, n_rows)), dma((2, 2, n_rows)), dma((5, 2)), dma((5, 2)),
                dma((6, 4)), dma((6, 4)), dma((6, 4)), dma((6, 4)),
                dma((2, 4)), dma((2, 4)), dma((2, 4)), dma((2, 4)),
                dma((2, 2)), dma((2, 2)), dma((2, 2, 2)), dma((2, 4)),
                dma((n_rows,)), dma((n_rows,)),
            ],
            compiler_params=pltpu.CompilerParams(collective_id=0, has_side_effects=True, vmem_limit_bytes=60 << 20),
            name="gmres",
        )(
            near_cols.T,
            far_src.reshape(n_rows),
            far_tgt.reshape(n_rows),
            right_side.reshape(CL_DEV, B, 2 * HALF),
            near_blocks,
            jnp.swapaxes(far_left.reshape(n_rows, B, R), 1, 2),
            jnp.swapaxes(far_right.reshape(n_rows, B, R), 1, 2),
        )
        sol, res = pl.pallas_call(
            deliver,
            out_shape=(jax.ShapeDtypeStruct((32, CL_DEV * B), F32),) * 2,
            in_specs=[vector] * 2,
            out_specs=(vector, vector),
            name="deliver",
        )(sol, res)
        return sol.T, res.T

    return jax.shard_map(
        shards,
        mesh=mesh,
        in_specs=(
            P("rows", None),
            P("rows", "far", None, None),
            P("rows", "far"),
            P("rows", None, "far"),
            P("rows", None, "far"),
            P("rows", None, "far", None, None),
            P("rows", None, "far", None, None),
        ),
        out_specs=(P("rows", "far"), P("rows", "far")),
        check_vma=False,
    )
```
